32 devices in a mesh: section: 4 (over y, x), dp: 2 (over core), mp: 4 (over z).
Axes of the slice: x: 2, y: 2, z: 4, core: 2. Of those that a mesh axis runs over, the one named last changes fastest.
Arguments:
- act_sent: bfloat16 [4, 16, 3072], P('section', ('dp', 'mp')), may hold values from -6 to 6
- new_batch: bfloat16 [16, 3072], P(('dp', 'mp')), may hold values from -6 to 6
- saved_input: bfloat16 [4, 16, 3072], P('section', ('dp', 'mp')), may hold values from -6 to 6
- grad_sent: bfloat16 [4, 16, 3072], P('section', ('dp', 'mp')), may hold values from -6 to 6
- loss_grad: bfloat16 [16, 3072], P(('dp', 'mp')), may hold values from -6 to 6
- ln_gain: float32 [4, 3072], P('section'), may hold values from 0.1 to 1.9
- w_in: bfloat16 [4, 3072, 16384], P('section', None, 'mp'), may hold values from -0.109375 to 0.109375
- w_out: bfloat16 [4, 3072, 16384], P('section', None, 'mp'), may hold values from -0.046875 to 0.046875
Outputs:
- act_out: bfloat16 [4, 16, 3072], P('section', ('dp', 'mp'))
- grad_out: bfloat16 [4, 16, 3072], P('section', ('dp', 'mp'))
- grad_w_in: bfloat16 [4, 3072, 16384], P('section', 'dp', 'mp')
- grad_w_out: bfloat16 [4, 3072, 16384], P('section', 'dp', 'mp')
The draws below stay inside these ranges and needn't reach their ends.
All inputs are finite; a program needn't handle non-finite values.
Results may differ from the reference program's by a relative error of at most 0.0075.
Values may be sent and summed in bfloat16 or wider, within the bound.
No kernel may reach another device: no remote copies, remote signals or barrier semaphores. Data moves between devices by JAX's collectives and lax.ppermute only.
A program may use at most 128 MiB of HBM per device.

```python
import jax
import jax.numpy as jnp
from jax import lax

D = 3072
FF = 16384
SECTIONS = 4
TOKENS = 16
N_DP = 2


def block_scale(stream_key, extent, split, least, high):
    loudness = 1.0
    for dim, shards_of in split:
        steps = jax.random.uniform(jax.random.fold_in(jax.random.fold_in(stream_key, 6), dim), (shards_of,), jnp.float32, least / len(split), high / len(split))
        loudness = loudness * jnp.repeat(jnp.exp(steps), extent[dim] // shards_of).reshape((-1,) + (1,) * (len(extent) - 1 - dim))
    return loudness


def normal_values(stream_key, shape, spread, most, shards=(), dtype=jnp.bfloat16):
    level = block_scale(stream_key, shape, shards, -0.22, 0.18) if shards else 1.0
    drawn = jax.random.normal(stream_key, shape, jnp.float32) * spread * level
    return jnp.minimum(jnp.maximum(drawn, -most), most).astype(dtype)


def setup_inputs(seed: int = 0) -> dict:
    keys = jax.random.split(jax.random.key(seed), 9)
    return {
        "act_sent": normal_values(keys[0], (SECTIONS, TOKENS, D), 1.0, 6.0, ((0, 4), (1, 8))),
        "new_batch": normal_values(keys[1], (TOKENS, D), 1.0, 6.0, ((0, 8),)),
        "saved_input": normal_values(keys[2], (SECTIONS, TOKENS, D), 1.0, 6.0, ((0, 4), (1, 8))),
        "grad_sent": normal_values(keys[3], (SECTIONS, TOKENS, D), 1.0, 6.0, ((0, 4), (1, 8))),
        "loss_grad": normal_values(keys[4], (TOKENS, D), 1.0, 6.0, ((0, 8),)),
        "ln_gain": jnp.clip(1.0 + 0.18 * jax.random.normal(keys[5], (SECTIONS, D), jnp.float32), 0.1, 1.9),
        "w_in": normal_values(keys[6], (SECTIONS, D, FF), D ** -0.5, 0.109375, ((0, 4), (2, 4))),
        "w_out": normal_values(keys[7], (SECTIONS, D, FF), FF ** -0.5, 0.046875, ((0, 4), (2, 4))),
    }


gelu_c = 0.7978845608028654

def gelu_pair(h):
    inner = gelu_c * (h + 0.044715 * h * h * h)
    tval = jnp.tanh(inner)
    value = 0.5 * h * (1.0 + tval)
    slope = 0.5 * (1.0 + tval) + 0.5 * h * (1.0 - tval * tval) * gelu_c * (1.0 + 3.0 * 0.044715 * h * h)
    return (value, slope)

def normalize(rows):
    xval = rows.astype(jnp.float32)
    centre = xval - lax.optimization_barrier(jnp.mean(xval, axis=-1, keepdims=True))
    rstd = lax.rsqrt(lax.optimization_barrier(jnp.mean(centre * centre, axis=-1, keepdims=True)) + 1e-05)
    return (centre * rstd, rstd)

def one_section(items):
    x_fwd, x_bwd, upstream, gain, weight_in, weight_out = items
    nhat_fwd, _ = normalize(x_fwd)
    n_fwd = (nhat_fwd * gain).astype(jnp.bfloat16)
    nhat_bwd, rstd_bwd = normalize(x_bwd)
    n_bwd = (nhat_bwd * gain).astype(jnp.bfloat16)
    h_fwd = jnp.dot(n_fwd, weight_in, preferred_element_type=jnp.float32)
    g_fwd = gelu_pair(h_fwd)[0].astype(jnp.bfloat16)
    branch = lax.dot_general(g_fwd, weight_out, (((1,), (1,)), ((), ())), preferred_element_type=jnp.float32)
    act = (x_fwd.astype(jnp.float32) + branch).astype(jnp.bfloat16)
    h_bwd = jnp.dot(n_bwd, weight_in, preferred_element_type=jnp.float32)
    g_val, slope = gelu_pair(h_bwd)
    g_bwd = g_val.astype(jnp.bfloat16)
    grad_act = jnp.dot(upstream, weight_out, preferred_element_type=jnp.float32)
    dh = (grad_act * slope).astype(jnp.bfloat16)
    dn = lax.dot_general(dh, weight_in, (((1,), (1,)), ((), ())), preferred_element_type=jnp.float32)
    scaled = dn * gain
    dx = upstream.astype(jnp.float32) + rstd_bwd * (scaled - lax.optimization_barrier(jnp.mean(scaled, axis=-1, keepdims=True)) - nhat_bwd * lax.optimization_barrier(jnp.mean(scaled * nhat_bwd, axis=-1, keepdims=True)))
    block = TOKENS // N_DP
    sum_in = jnp.zeros(weight_in.shape, jnp.float32)
    sum_out = jnp.zeros(weight_out.shape, jnp.float32)
    for replica in range(N_DP):
        lo = replica * block
        part_in = lax.dot_general(n_bwd[lo:lo + block], dh[lo:lo + block], (((0,), (0,)), ((), ())), preferred_element_type=jnp.float32)
        part_out = lax.dot_general(upstream[lo:lo + block], g_bwd[lo:lo + block], (((0,), (0,)), ((), ())), preferred_element_type=jnp.float32)
        sum_in = sum_in + part_in.astype(jnp.bfloat16).astype(jnp.float32)
        sum_out = sum_out + part_out.astype(jnp.bfloat16).astype(jnp.float32)
    return (act, dx.astype(jnp.bfloat16), sum_in.astype(jnp.bfloat16), sum_out.astype(jnp.bfloat16))

def reference(act_sent, new_batch, saved_input, grad_sent, loss_grad, ln_gain, w_in, w_out):
    x_fwd = jnp.concatenate([new_batch[None], act_sent[:-1]], axis=0)
    upstream = jnp.concatenate([grad_sent[1:], loss_grad[None]], axis=0)
    return lax.map(one_section, (x_fwd, saved_input, upstream, ln_gain, w_in, w_out))
```

```python
import functools

import jax
import jax.numpy as jnp
from jax import lax
from jax.experimental import pallas as pl
from jax.experimental.pallas import tpu as pltpu
from jax.sharding import PartitionSpec as P

GELU_C = 0.7978845608028654
BF16 = jnp.bfloat16
F32 = jnp.float32
MIB = 1 << 20


def gelu_value(h):
    tval = jnp.tanh(GELU_C * (h + 0.044715 * h * h * h))
    return 0.5 * h * (1.0 + tval)


def gelu_pair(h):
    tval = jnp.tanh(GELU_C * (h + 0.044715 * h * h * h))
    value = 0.5 * h * (1.0 + tval)
    slope = 0.5 * (1.0 + tval) + 0.5 * h * (1.0 - tval * tval) * GELU_C * (
        1.0 + 3.0 * 0.044715 * h * h
    )
    return value, slope


def normalize(xval):
    centre = xval - jnp.mean(xval, axis=-1, keepdims=True)
    rstd = lax.rsqrt(jnp.mean(centre * centre, axis=-1, keepdims=True) + 1e-05)
    return centre * rstd, rstd


def contract_last(left, right):
    return lax.dot_general(
        left, right, (((1,), (1,)), ((), ())), preferred_element_type=F32
    )


def contract_first(left, right):
    return lax.dot_general(
        left, right, (((0,), (0,)), ((), ())), preferred_element_type=F32
    )


def block_kernel(sections, dp, chunks, where_ref, *refs):
    rows_refs = refs[:dp]
    gain_ref, win_hbm, wout_hbm = refs[dp : dp + 3]
    hid_ref, part_ref, norm_ref, up_ref = refs[dp + 3 : dp + 7]
    both, win, wout, branch, dnorm, sem_in, sem_out = refs[dp + 7 :]
    section, replica = where_ref[0], where_ref[1]
    block = rows_refs[0].shape[1]
    tokens = dp * block
    hidden = win.shape[1]
    width = hidden // chunks
    start = replica * hidden

    def fetch(source, target, sem, chunk):
        columns = pl.ds(pl.multiple_of(start + chunk * width, width), width)
        return pltpu.make_async_copy(
            source.at[:, columns], target.at[:, pl.ds(chunk * width, width)], sem.at[chunk]
        )

    for chunk in range(chunks):
        fetch(win_hbm, win, sem_in, chunk).start()
        fetch(wout_hbm, wout, sem_out, chunk).start()

    behind = lax.rem(section + sections - 1, sections)
    ahead = lax.rem(section + 1, sections)
    gain = gain_ref[...]

    def rows_of(slot, owner):
        rows = rows_refs[0][slot]
        for k in range(1, dp):
            rows = jnp.where(
                lax.rem(replica + dp - k, dp) == owner, rows_refs[k][slot], rows
            )
        return rows

    for owner in range(dp):
        low = owner * block
        nhat, _ = normalize(rows_of(behind, owner).astype(F32))
        both[low : low + block, :] = (nhat * gain).astype(BF16)
        nhat, _ = normalize(rows_of(section, owner).astype(F32))
        n_bwd = (nhat * gain).astype(BF16)
        both[tokens + low : tokens + low + block, :] = n_bwd
        norm_ref[low : low + block, :] = n_bwd
        up_ref[low : low + block, :] = rows_of(ahead, owner)

    def first(chunk):
        columns = slice(chunk * width, (chunk + 1) * width)
        fetch(win_hbm, win, sem_in, chunk).wait()
        h = jnp.dot(both[...], win[:, columns], preferred_element_type=F32)
        fetch(wout_hbm, wout, sem_out, chunk).wait()
        grad_act = jnp.dot(up_ref[...], wout[:, columns], preferred_element_type=F32)
        g_fwd = gelu_value(h[:tokens]).astype(BF16)
        g_bwd, slope = gelu_pair(h[tokens:])
        dh = (grad_act * slope).astype(BF16)
        hid_ref[0, :, columns] = dh
        hid_ref[1, :, columns] = g_bwd.astype(BF16)
        return g_fwd, dh

    def second(chunk, g_fwd, dh):
        columns = slice(chunk * width, (chunk + 1) * width)
        term_n = contract_last(dh, win[:, columns])
        term_b = contract_last(g_fwd, wout[:, columns])
        if chunk == 0:
            dnorm[...] = term_n
            branch[...] = term_b
        else:
            dnorm[...] += term_n
            branch[...] += term_b

    pending = first(0)
    for chunk in range(1, chunks):
        later = first(chunk)
        second(chunk - 1, *pending)
        pending = later
    second(chunks - 1, *pending)

    owners, mine = part_ref.shape[0], part_ref.shape[1] // 2
    for owner in range(owners):
        rows = slice(owner * mine, (owner + 1) * mine)
        part_ref[owner, :mine, :] = branch[rows, :].astype(BF16)
        part_ref[owner, mine:, :] = dnorm[rows, :].astype(BF16)


def weight_kernel(where_ref, norm_ref, up_ref, hid_ref, *refs):
    in_ref, out_ref = refs[-2:]
    in_ref[...] = contract_first(norm_ref[...], hid_ref[0]).astype(BF16)
    out_ref[...] = contract_first(up_ref[...], hid_ref[1]).astype(BF16)


def finish_kernel(sections, mp, where_ref, recv_ref, rows_ref, saved_ref, gain_ref, act_ref, grad_ref):
    section, lane = where_ref[0], where_ref[2]
    mine = saved_ref.shape[1]
    total = jnp.sum(recv_ref[...].astype(F32), axis=0)
    behind = lax.rem(section + sections - 1, sections) * mp + lane
    ahead = lax.rem(section + 1, sections) * mp + lane
    act_ref[0] = (rows_ref[behind].astype(F32) + total[:mine]).astype(BF16)
    nhat, rstd = normalize(saved_ref[0].astype(F32))
    scaled = total[mine:] * gain_ref[...]
    grad = rows_ref[ahead].astype(F32) + rstd * (
        scaled
        - jnp.mean(scaled, axis=-1, keepdims=True)
        - nhat * jnp.mean(scaled * nhat, axis=-1, keepdims=True)
    )
    grad_ref[0] = grad.astype(BF16)


def divisor(size, most):
    return max(k for k in range(1, most + 1) if size % k == 0)


def per_device(sections, dp, mp, act_sent, new_batch, saved_input, grad_sent, loss_grad, ln_gain, w_in, w_out):
    section = lax.axis_index("section")
    replica = lax.axis_index("dp")
    lane = lax.axis_index("mp")
    where = jnp.stack([section, replica, lane]).astype(jnp.int32)
    mine, width = new_batch.shape
    hidden = w_in.shape[2] // dp
    block = mp * mine
    tokens = dp * block
    vmem = pl.BlockSpec(memory_space=pltpu.VMEM)
    smem = pl.BlockSpec(memory_space=pltpu.SMEM)
    hbm = pl.BlockSpec(memory_space=pl.ANY)

    to_next = jnp.where(section == sections - 1, new_batch, act_sent[0])
    to_last = jnp.where(section == 0, loss_grad, grad_sent[0])
    step = ((jnp.arange(sections) - section) % sections)[:, None, None, None]
    sent = jnp.where(step == 0, saved_input[0], jnp.where(step == 1, to_next, to_last))
    sent = jnp.broadcast_to(sent, (sections, mp, mine, width)).reshape(sections * mp, mine, width)
    got = lax.all_to_all(sent, ("section", "mp"), 0, 0)
    own = got.reshape(sections, block, width)
    rows = [own] + [
        lax.ppermute(own, "dp", [(i, (i + k) % dp) for i in range(dp)]) for k in range(1, dp)
    ]

    chunks = divisor(hidden // 128, 4)
    hid, part, n_bwd, upstream = pl.pallas_call(
        functools.partial(block_kernel, sections, dp, chunks),
        in_specs=[smem] + [vmem] * dp + [vmem, hbm, hbm],
        out_specs=[vmem] * 4,
        out_shape=[
            jax.ShapeDtypeStruct((2, tokens, hidden), BF16),
            jax.ShapeDtypeStruct((dp * mp, 2 * mine, width), BF16),
            jax.ShapeDtypeStruct((tokens, width), BF16),
            jax.ShapeDtypeStruct((tokens, width), BF16),
        ],
        scratch_shapes=[
            pltpu.VMEM((2 * tokens, width), BF16),
            pltpu.VMEM((width, hidden), BF16),
            pltpu.VMEM((width, hidden), BF16),
            pltpu.VMEM((tokens, width), F32),
            pltpu.VMEM((tokens, width), F32),
            pltpu.SemaphoreType.DMA((chunks,)),
            pltpu.SemaphoreType.DMA((chunks,)),
        ],
        compiler_params=pltpu.CompilerParams(vmem_limit_bytes=44 * MIB),
        cost_estimate=pl.CostEstimate(
            flops=12 * tokens * width * hidden, bytes_accessed=4 * width * hidden, transcendentals=2 * tokens * hidden
        ),
        name="block",
    )(where, *rows, ln_gain, w_in[0], w_out[0])

    hids = [hid] + [
        lax.ppermute(hid, "dp", [(i, (i + k) % dp) for i in range(dp)]) for k in range(1, dp)
    ]
    recv = lax.all_to_all(part, ("dp", "mp"), 0, 0)

    half = width // dp
    tile = 128 * divisor(half // 128, max(1, 6 * 2048 // hidden))
    steps = half // tile
    grads = []
    for k in range(dp):
        grads = pl.pallas_call(
            weight_kernel,
            grid_spec=pltpu.PrefetchScalarGridSpec(
                num_scalar_prefetch=1,
                grid=(steps,),
                in_specs=[
                    pl.BlockSpec((tokens, tile), lambda i, w: (0, w[1] * steps + i)),
                    pl.BlockSpec((tokens, tile), lambda i, w: (0, w[1] * steps + i)),
                    pl.BlockSpec((2, tokens, hidden), lambda i, w: (0, 0, 0)),
                ]
                + [hbm] * len(grads),
                out_specs=[
                    pl.BlockSpec((tile, hidden), lambda i, w, k=k: (i, lax.rem(w[1] + dp - k, dp)))
                ]
                * 2,
            ),
            out_shape=[jax.ShapeDtypeStruct((half, dp * hidden), BF16)] * 2,
            input_output_aliases={4: 0, 5: 1} if grads else {},
            compiler_params=pltpu.CompilerParams(vmem_limit_bytes=32 * MIB),
            cost_estimate=pl.CostEstimate(
                flops=4 * tokens * half * hidden, bytes_accessed=4 * half * hidden, transcendentals=0
            ),
            name="weight",
        )(where, n_bwd, upstream, hids[k], *grads)

    act_out, grad_out = pl.pallas_call(
        functools.partial(finish_kernel, sections, mp),
        in_specs=[smem] + [vmem] * 4,
        out_specs=[vmem] * 2,
        out_shape=[jax.ShapeDtypeStruct((1, mine, width), BF16)] * 2,
        compiler_params=pltpu.CompilerParams(vmem_limit_bytes=16 * MIB),
        name="finish",
    )(where, recv, got, saved_input, ln_gain)
    return act_out, grad_out, grads[0][None], grads[1][None]


def solution(mesh):
    sizes = dict(mesh.shape)
    body = functools.partial(per_device, sizes["section"], sizes["dp"], sizes["mp"])
    return jax.shard_map(
        body,
        mesh=mesh,
        in_specs=(
            P("section", ("dp", "mp"), None),
            P(("dp", "mp"), None),
            P("section", ("dp", "mp"), None),
            P("section", ("dp", "mp"), None),
            P(("dp", "mp"), None),
            P("section", None),
            P("section", None, "mp"),
            P("section", None, "mp"),
        ),
        out_specs=(
            P("section", ("dp", "mp"), None),
            P("section", ("dp", "mp"), None),
            P("section", "dp", "mp"),
            P("section", "dp", "mp"),
        ),
        check_vma=False,
    )
```

```python
import functools

import jax
import jax.numpy as jnp
from jax import lax
from jax.experimental import pallas as pl
from jax.experimental.pallas import tpu as pltpu
from jax.sharding import PartitionSpec as P


GELU_C = 0.7978845608028654
BF16 = jnp.bfloat16
F32 = jnp.float32
MIB = 1 << 20


def gelu_value(h):
    tval = jnp.tanh(GELU_C * (h + 0.044715 * h * h * h))
    return 0.5 * h * (1.0 + tval)


def gelu_pair(h):
    tval = jnp.tanh(GELU_C * (h + 0.044715 * h * h * h))
    value = 0.5 * h * (1.0 + tval)
    slope = 0.5 * (1.0 + tval) + 0.5 * h * (1.0 - tval * tval) * GELU_C * (
        1.0 + 3.0 * 0.044715 * h * h
    )
    return value, slope


def normalize(xval):
    centre = xval - jnp.mean(xval, axis=-1, keepdims=True)
    rstd = lax.rsqrt(jnp.mean(centre * centre, axis=-1, keepdims=True) + 1e-05)
    return centre * rstd, rstd


def contract_last(left, right):
    return lax.dot_general(
        left, right, (((1,), (1,)), ((), ())), preferred_element_type=F32
    )


def contract_first(left, right):
    return lax.dot_general(
        left, right, (((0,), (0,)), ((), ())), preferred_element_type=F32
    )


def send_kernel(sections, mp, where_ref, act_ref, batch_ref, saved_ref, grad_ref, loss_ref, sent_ref, sems):
    section = where_ref[0]
    behind = lax.rem(section + sections - 1, sections)
    ahead = lax.rem(section + 1, sections)

    def spread(source, target, sem):
        def start(lane, carry):
            pltpu.make_async_copy(source, sent_ref.at[target * mp + lane], sems.at[sem]).start()
            return carry

        lax.fori_loop(0, mp, start, 0, unroll=mp <= 8)

    spread(saved_ref.at[0], section, 0)

    @pl.when(section == sections - 1)
    def _():
        spread(batch_ref, ahead, 1)

    @pl.when(section != sections - 1)
    def _():
        spread(act_ref.at[0], ahead, 1)

    @pl.when(section == 0)
    def _():
        spread(loss_ref, behind, 2)

    @pl.when(section != 0)
    def _():
        spread(grad_ref.at[0], behind, 2)

    for sem in range(3):
        whole = sent_ref.at[pl.ds(0, mp)]
        pltpu.make_async_copy(whole, whole, sems.at[sem]).wait()


def block_kernel(sections, dp, chunks, depth, where_ref, *refs):
    rows_refs = refs[:dp]
    gain_hbm, win_hbm, wout_hbm = refs[dp : dp + 3]
    hid_ref, part_ref, norm_ref, up_ref = refs[dp + 3 : dp + 7]
    both, gain_ref, win, wout, branch, dnorm, sem_gain, sem_in, sem_out = refs[dp + 7 :]
    section, replica = where_ref[0], where_ref[1]
    block = rows_refs[0].shape[1]
    tokens = dp * block
    hidden = win.shape[1]
    width = hidden // chunks
    start = replica * hidden

    def fetch(chunk):
        source = pl.ds(pl.multiple_of(start + chunk * width, 128), width)
        target = pl.ds(chunk * width, width)
        return (
            pltpu.make_async_copy(win_hbm.at[:, source], win.at[:, target], sem_in.at[chunk]),
            pltpu.make_async_copy(wout_hbm.at[:, source], wout.at[:, target], sem_out.at[chunk]),
        )

    fetch_gain = pltpu.make_async_copy(gain_hbm, gain_ref, sem_gain)
    fetch_gain.start()
    for chunk in range(min(depth, chunks)):
        for copy in fetch(chunk):
            copy.start()

    behind = lax.rem(section + sections - 1, sections)
    ahead = lax.rem(section + 1, sections)
    fetch_gain.wait()
    gain = gain_ref[...]

    def rows_of(slot, owner):
        rows = rows_refs[0][slot]
        for k in range(1, dp):
            rows = jnp.where(
                lax.rem(replica + dp - k, dp) == owner, rows_refs[k][slot], rows
            )
        return rows

    for owner in range(dp):
        low = owner * block
        nhat, _ = normalize(rows_of(behind, owner).astype(F32))
        both[low : low + block, :] = (nhat * gain).astype(BF16)
        nhat, _ = normalize(rows_of(section, owner).astype(F32))
        n_bwd = (nhat * gain).astype(BF16)
        both[tokens + low : tokens + low + block, :] = n_bwd
        norm_ref[low : low + block, :] = n_bwd
        up_ref[low : low + block, :] = rows_of(ahead, owner)

    def first(chunk):
        columns = slice(chunk * width, (chunk + 1) * width)
        for copy in fetch(chunk):
            copy.wait()
        if chunk + depth < chunks:
            for copy in fetch(chunk + depth):
                copy.start()
        h = jnp.dot(both[...], win[:, columns], preferred_element_type=F32)
        grad_act = jnp.dot(up_ref[...], wout[:, columns], preferred_element_type=F32)
        g_fwd = gelu_value(h[:tokens]).astype(BF16)
        g_bwd, slope = gelu_pair(h[tokens:])
        dh = (grad_act * slope).astype(BF16)
        hid_ref[0, :, columns] = dh
        hid_ref[1, :, columns] = g_bwd.astype(BF16)
        return g_fwd, dh

    def second(chunk, g_fwd, dh):
        columns = slice(chunk * width, (chunk + 1) * width)
        term_n = contract_last(dh, win[:, columns])
        term_b = contract_last(g_fwd, wout[:, columns])
        if chunk == 0:
            dnorm[...] = term_n
            branch[...] = term_b
        else:
            dnorm[...] += term_n
            branch[...] += term_b

    pending = first(0)
    for chunk in range(1, chunks):
        later = first(chunk)
        second(chunk - 1, *pending)
        pending = later
    second(chunks - 1, *pending)

    owners, mine = part_ref.shape[0], part_ref.shape[1] // 2
    for owner in range(owners):
        rows = slice(owner * mine, (owner + 1) * mine)
        part_ref[owner, :mine, :] = branch[rows, :].astype(BF16)
        part_ref[owner, mine:, :] = dnorm[rows, :].astype(BF16)


def weight_kernel(dp, tile, where_ref, norm_ref, up_ref, *refs):
    hid_refs = refs[:dp]
    targets, buffers, sems = refs[dp : dp + 2], refs[dp + 2 : dp + 4], refs[dp + 4]
    replica = where_ref[1]
    half = buffers[0].shape[0]
    hidden = hid_refs[0].shape[2]
    copies = []
    for k in range(dp):
        there = pl.ds(pl.multiple_of(lax.rem(replica + dp - k, dp) * hidden, 128), hidden)
        here = pl.ds(k * hidden, hidden)
        for step in range(half // tile):
            rows = pl.ds(step * tile, tile)
            columns = pl.ds(pl.multiple_of(replica * half + step * tile, 128), tile)
            for which, left in enumerate((norm_ref, up_ref)):
                buffer = buffers[which]
                buffer[rows, here] = contract_first(left[:, columns], hid_refs[k][which]).astype(BF16)
                copy = pltpu.make_async_copy(
                    buffer.at[rows, here], targets[which].at[rows, there], sems.at[len(copies)]
                )
                copy.start()
                copies.append(copy)
    for copy in copies:
        copy.wait()


def finish_kernel(sections, mp, where_ref, recv_ref, rows_ref, saved_ref, gain_ref, act_ref, grad_ref):
    section, lane = where_ref[0], where_ref[2]
    mine = saved_ref.shape[1]
    total = jnp.sum(recv_ref[...].astype(F32), axis=0)
    behind = lax.rem(section + sections - 1, sections) * mp + lane
    ahead = lax.rem(section + 1, sections) * mp + lane
    act_ref[0] = (rows_ref[behind].astype(F32) + total[:mine]).astype(BF16)
    nhat, rstd = normalize(saved_ref[0].astype(F32))
    scaled = total[mine:] * gain_ref[...]
    grad = rows_ref[ahead].astype(F32) + rstd * (
        scaled
        - jnp.mean(scaled, axis=-1, keepdims=True)
        - nhat * jnp.mean(scaled * nhat, axis=-1, keepdims=True)
    )
    grad_ref[0] = grad.astype(BF16)


def divisor(size, most):
    return max(k for k in range(1, most + 1) if size % k == 0)


def per_device(sections, dp, mp, act_sent, new_batch, saved_input, grad_sent, loss_grad, ln_gain, w_in, w_out):
    section = lax.axis_index("section")
    replica = lax.axis_index("dp")
    lane = lax.axis_index("mp")
    where = jnp.stack([section, replica, lane]).astype(jnp.int32)
    mine, width = new_batch.shape
    hidden = w_in.shape[2] // dp
    block = mp * mine
    tokens = dp * block
    vmem = pl.BlockSpec(memory_space=pltpu.VMEM)
    smem = pl.BlockSpec(memory_space=pltpu.SMEM)
    hbm = pl.BlockSpec(memory_space=pltpu.HBM)

    params = lambda mib: pltpu.CompilerParams(vmem_limit_bytes=mib * MIB)
    stay = lambda *arrays: [pltpu.with_memory_space_constraint(x, pltpu.HBM) for x in arrays]
    like = jax.ShapeDtypeStruct
    sent = pl.pallas_call(
        functools.partial(send_kernel, sections, mp),
        in_specs=[smem] + [hbm] * 5,
        out_specs=vmem,
        out_shape=like((sections * mp, mine, width), BF16),
        scratch_shapes=[pltpu.SemaphoreType.DMA((3,))],
        compiler_params=params(4),
        name="send",
    )(where, *stay(act_sent, new_batch, saved_input, grad_sent, loss_grad))
    got = lax.all_to_all(sent, ("section", "mp"), 0, 0)
    own = got.reshape(sections, block, width)
    rows = [own] + [
        lax.ppermute(own, "dp", [(i, (i + k) % dp) for i in range(dp)]) for k in range(1, dp)
    ]

    chunks = divisor(hidden // 128, 8)
    hid, part, n_bwd, upstream = pl.pallas_call(
        functools.partial(block_kernel, sections, dp, chunks, 3),
        in_specs=[smem] + [vmem] * dp + [hbm] * 3,
        out_specs=[vmem] * 4,
        out_shape=[
            like((2, tokens, hidden), BF16),
            like((dp * mp, 2 * mine, width), BF16),
            like((tokens, width), BF16),
            like((tokens, width), BF16),
        ],
        scratch_shapes=[
            pltpu.VMEM((2 * tokens, width), BF16),
            pltpu.VMEM((1, width), F32),
            pltpu.VMEM((width, hidden), BF16),
            pltpu.VMEM((width, hidden), BF16),
            pltpu.VMEM((tokens, width), F32),
            pltpu.VMEM((tokens, width), F32),
            pltpu.SemaphoreType.DMA,
            pltpu.SemaphoreType.DMA((chunks,)),
            pltpu.SemaphoreType.DMA((chunks,)),
        ],
        compiler_params=params(36),
        cost_estimate=pl.CostEstimate(
            flops=12 * tokens * width * hidden, bytes_accessed=4 * width * hidden, transcendentals=2 * tokens * hidden
        ),
        name="block",
    )(where, *rows, *stay(ln_gain, w_in[0], w_out[0]))

    hids = [hid] + [
        lax.ppermute(hid, "dp", [(i, (i + k) % dp) for i in range(dp)]) for k in range(1, dp)
    ]
    recv = lax.all_to_all(part, ("dp", "mp"), 0, 0)

    half = width // dp
    tile = 128 * divisor(half // 128, 2)
    grads = pl.pallas_call(
        functools.partial(weight_kernel, dp, tile),
        in_specs=[smem] + [vmem] * (2 + dp),
        out_specs=[hbm] * 2,
        out_shape=[like((half, dp * hidden), BF16)] * 2,
        scratch_shapes=[
            pltpu.VMEM((half, dp * hidden), BF16),
            pltpu.VMEM((half, dp * hidden), BF16),
            pltpu.SemaphoreType.DMA((2 * dp * (half // tile),)),
        ],
        compiler_params=params(36),
        cost_estimate=pl.CostEstimate(
            flops=4 * tokens * half * hidden * dp, bytes_accessed=4 * half * hidden * dp, transcendentals=0
        ),
        name="weight",
    )(where, n_bwd, upstream, *hids)

    act_out, grad_out = pl.pallas_call(
        functools.partial(finish_kernel, sections, mp),
        in_specs=[smem] + [vmem] * 4,
        out_specs=[vmem] * 2,
        out_shape=[like((1, mine, width), BF16)] * 2,
        compiler_params=params(16),
        name="finish",
    )(where, recv, got, saved_input, ln_gain)
    return act_out, grad_out, grads[0][None], grads[1][None]


def solution(mesh):
    sizes = dict(mesh.shape)
    body = functools.partial(per_device, sizes["section"], sizes["dp"], sizes["mp"])
    return jax.shard_map(
        body,
        mesh=mesh,
        in_specs=(
            P("section", ("dp", "mp"), None),
            P(("dp", "mp"), None),
            P("section", ("dp", "mp"), None),
            P("section", ("dp", "mp"), None),
            P(("dp", "mp"), None),
            P("section", None),
            P("section", None, "mp"),
            P("section", None, "mp"),
        ),
        out_specs=(
            P("section", ("dp", "mp"), None),
            P("section", ("dp", "mp"), None),
            P("section", "dp", "mp"),
            P("section", "dp", "mp"),
        ),
        check_vma=False,
    )
```

```python
import functools

import jax
import jax.numpy as jnp
from jax import lax
from jax.experimental import pallas as pl
from jax.experimental.pallas import tpu as pltpu
from jax.sharding import PartitionSpec as P


GELU_C = 0.7978845608028654
BF16 = jnp.bfloat16
F32 = jnp.float32
MIB = 1 << 20


def gelu_value(h):
    tval = jnp.tanh(GELU_C * (h + 0.044715 * h * h * h))
    return 0.5 * h * (1.0 + tval)


def gelu_pair(h):
    tval = jnp.tanh(GELU_C * (h + 0.044715 * h * h * h))
    value = 0.5 * h * (1.0 + tval)
    slope = 0.5 * (1.0 + tval) + 0.5 * h * (1.0 - tval * tval) * GELU_C * (
        1.0 + 3.0 * 0.044715 * h * h
    )
    return value, slope


def normalize(xval):
    centre = xval - jnp.mean(xval, axis=-1, keepdims=True)
    rstd = lax.rsqrt(jnp.mean(centre * centre, axis=-1, keepdims=True) + 1e-05)
    return centre * rstd, rstd


def contract_last(left, right):
    return lax.dot_general(
        left, right, (((1,), (1,)), ((), ())), preferred_element_type=F32
    )


def contract_first(left, right):
    return lax.dot_general(
        left, right, (((0,), (0,)), ((), ())), preferred_element_type=F32
    )


def send_kernel(sections, dp, mp, where_ref, act_ref, batch_ref, saved_ref, grad_ref, loss_ref, gain_hbm, win_hbm, wout_hbm, sent_ref, gain_ref, win_ref, wout_ref, sems, near):
    section = where_ref[0]
    width = win_ref.shape[1]
    columns = pl.ds(pl.multiple_of(where_ref[1] * (win_hbm.shape[1] // dp), 128), width)
    behind = lax.rem(section + sections - 1, sections)
    ahead = lax.rem(section + 1, sections)

    def spread(source, target, sem):
        def start(lane, carry):
            pltpu.make_async_copy(source, sent_ref.at[target * mp + lane], sems.at[sem]).start()
            return carry

        lax.fori_loop(0, mp, start, 0, unroll=mp <= 8)

    spread(saved_ref.at[0], section, 0)

    @pl.when(section == sections - 1)
    def _():
        spread(batch_ref, ahead, 1)

    @pl.when(section != sections - 1)
    def _():
        spread(act_ref.at[0], ahead, 1)

    @pl.when(section == 0)
    def _():
        spread(loss_ref, behind, 2)

    @pl.when(section != 0)
    def _():
        spread(grad_ref.at[0], behind, 2)

    early = [
        pltpu.make_async_copy(gain_hbm, gain_ref, near.at[0]),
        pltpu.make_async_copy(win_hbm.at[:, columns], win_ref, near.at[1]),
        pltpu.make_async_copy(wout_hbm.at[:, columns], wout_ref, near.at[2]),
    ]
    for copy in early:
        copy.start()
    for sem in range(3):
        whole = sent_ref.at[pl.ds(0, mp)]
        pltpu.make_async_copy(whole, whole, sems.at[sem]).wait()
    for copy in early:
        copy.wait()


def block_kernel(sections, dp, chunks, depth, where_ref, *refs):
    rows_refs = refs[:dp]
    gain_ref, win_first, wout_first, win_hbm, wout_hbm = refs[dp : dp + 5]
    hid_ref, part_ref, norm_ref, up_ref = refs[dp + 5 : dp + 9]
    both, win, wout, branch, dnorm, sem_in, sem_out = refs[dp + 9 :]
    section, replica = where_ref[0], where_ref[1]
    lanes = rows_refs[0].shape[0] // sections
    block = lanes * rows_refs[0].shape[1]
    tokens = dp * block
    width = win_first.shape[1]
    hidden = chunks * width
    start = replica * hidden

    def fetch(chunk):
        source = pl.ds(pl.multiple_of(start + chunk * width, 128), width)
        target = pl.ds((chunk - 1) * width, width)
        return (
            pltpu.make_async_copy(win_hbm.at[:, source], win.at[:, target], sem_in.at[chunk - 1]),
            pltpu.make_async_copy(wout_hbm.at[:, source], wout.at[:, target], sem_out.at[chunk - 1]),
        )

    for chunk in range(1, min(depth + 1, chunks)):
        for copy in fetch(chunk):
            copy.start()

    behind = lax.rem(section + sections - 1, sections)
    ahead = lax.rem(section + 1, sections)
    gain = gain_ref[...]

    def rows_of(slot, owner):
        here = pl.ds(slot * lanes, lanes)
        rows = rows_refs[0][here]
        for k in range(1, dp):
            rows = jnp.where(
                lax.rem(replica + dp - k, dp) == owner, rows_refs[k][here], rows
            )
        return rows.reshape(block, rows.shape[-1])

    def weights(chunk):
        if chunk == 0:
            return win_first[...], wout_first[...]
        columns = slice((chunk - 1) * width, chunk * width)
        return win[:, columns], wout[:, columns]

    for owner in range(dp):
        low = owner * block
        nhat, _ = normalize(rows_of(behind, owner).astype(F32))
        both[low : low + block, :] = (nhat * gain).astype(BF16)
        nhat, _ = normalize(rows_of(section, owner).astype(F32))
        n_bwd = (nhat * gain).astype(BF16)
        both[tokens + low : tokens + low + block, :] = n_bwd
        norm_ref[low : low + block, :] = n_bwd
        up_ref[low : low + block, :] = rows_of(ahead, owner)

    def first(chunk):
        columns = slice(chunk * width, (chunk + 1) * width)
        if chunk > 0:
            for copy in fetch(chunk):
                copy.wait()
            if chunk + depth < chunks:
                for copy in fetch(chunk + depth):
                    copy.start()
        w_in, w_out = weights(chunk)
        h = jnp.dot(both[...], w_in, preferred_element_type=F32)
        grad_act = jnp.dot(up_ref[...], w_out, preferred_element_type=F32)
        g_fwd = gelu_value(h[:tokens]).astype(BF16)
        g_bwd, slope = gelu_pair(h[tokens:])
        dh = (grad_act * slope).astype(BF16)
        hid_ref[0, :, columns] = dh
        hid_ref[1, :, columns] = g_bwd.astype(BF16)
        return g_fwd, dh

    def second(chunk, g_fwd, dh):
        w_in, w_out = weights(chunk)
        term_n = contract_last(dh, w_in)
        term_b = contract_last(g_fwd, w_out)
        if chunk == 0:
            dnorm[...] = term_n
            branch[...] = term_b
        else:
            dnorm[...] += term_n
            branch[...] += term_b

    pending = first(0)
    for chunk in range(1, chunks):
        later = first(chunk)
        second(chunk - 1, *pending)
        pending = later
    second(chunks - 1, *pending)

    owners, mine = part_ref.shape[0], part_ref.shape[1] // 2
    for owner in range(owners):
        rows = slice(owner * mine, (owner + 1) * mine)
        part_ref[owner, :mine, :] = branch[rows, :].astype(BF16)
        part_ref[owner, mine:, :] = dnorm[rows, :].astype(BF16)


def weight_kernel(dp, tile, where_ref, norm_ref, up_ref, *refs):
    hid_refs = refs[:dp]
    targets, buffers, sems = refs[dp : dp + 2], refs[dp + 2 : dp + 4], refs[dp + 4]
    replica = where_ref[1]
    half = buffers[0].shape[0]
    hidden = hid_refs[0].shape[2]
    copies = []
    for k in range(dp):
        there = pl.ds(pl.multiple_of(lax.rem(replica + dp - k, dp) * hidden, 128), hidden)
        here = pl.ds(k * hidden, hidden)
        for step in range(half // tile):
            rows = pl.ds(step * tile, tile)
            columns = pl.ds(pl.multiple_of(replica * half + step * tile, 128), tile)
            for which, left in enumerate((norm_ref, up_ref)):
                buffer = buffers[which]
                buffer[rows, here] = contract_first(left[:, columns], hid_refs[k][which]).astype(BF16)
                copy = pltpu.make_async_copy(
                    buffer.at[rows, here], targets[which].at[rows, there], sems.at[len(copies)]
                )
                copy.start()
                copies.append(copy)
    for copy in copies:
        copy.wait()


def finish_kernel(sections, mp, where_ref, recv_ref, rows_ref, saved_ref, gain_ref, act_ref, grad_ref):
    section, lane = where_ref[0], where_ref[2]
    mine = saved_ref.shape[1]
    total = jnp.sum(recv_ref[...].astype(F32), axis=0)
    behind = lax.rem(section + sections - 1, sections) * mp + lane
    ahead = lax.rem(section + 1, sections) * mp + lane
    act_ref[0] = (rows_ref[behind].astype(F32) + total[:mine]).astype(BF16)
    nhat, rstd = normalize(saved_ref[0].astype(F32))
    scaled = total[mine:] * gain_ref[...]
    grad = rows_ref[ahead].astype(F32) + rstd * (
        scaled
        - jnp.mean(scaled, axis=-1, keepdims=True)
        - nhat * jnp.mean(scaled * nhat, axis=-1, keepdims=True)
    )
    grad_ref[0] = grad.astype(BF16)


def divisor(size, most):
    return max(k for k in range(1, most + 1) if size % k == 0)


def per_device(sections, dp, mp, act_sent, new_batch, saved_input, grad_sent, loss_grad, ln_gain, w_in, w_out):
    section = lax.axis_index("section")
    replica = lax.axis_index("dp")
    lane = lax.axis_index("mp")
    where = jnp.stack([section, replica, lane]).astype(jnp.int32)
    mine, width = new_batch.shape
    hidden = w_in.shape[2] // dp
    block = mp * mine
    tokens = dp * block
    vmem = pl.BlockSpec(memory_space=pltpu.VMEM)
    smem = pl.BlockSpec(memory_space=pltpu.SMEM)
    hbm = pl.BlockSpec(memory_space=pltpu.HBM)

    params = lambda mib: pltpu.CompilerParams(vmem_limit_bytes=mib * MIB)
    stay = lambda *arrays: [pltpu.with_memory_space_constraint(x, pltpu.HBM) for x in arrays]
    like = jax.ShapeDtypeStruct
    chunks = divisor(hidden // 128, 8)
    first = hidden // chunks
    sent, gain, win, wout = pl.pallas_call(
        functools.partial(send_kernel, sections, dp, mp),
        in_specs=[smem] + [hbm] * 8,
        out_specs=[vmem] * 4,
        out_shape=[
            like((sections * mp, mine, width), BF16),
            like((1, width), F32),
            like((width, first), BF16),
            like((width, first), BF16),
        ],
        scratch_shapes=[pltpu.SemaphoreType.DMA((3,)), pltpu.SemaphoreType.DMA((3,))],
        compiler_params=params(4),
        name="send",
    )(where, *stay(act_sent, new_batch, saved_input, grad_sent, loss_grad, ln_gain, w_in[0], w_out[0]))
    got = lax.all_to_all(sent, ("section", "mp"), 0, 0)
    rows = [got] + [
        lax.ppermute(got, "dp", [(i, (i + k) % dp) for i in range(dp)]) for k in range(1, dp)
    ]

    rest = max(hidden - first, 128)
    hid, part, n_bwd, upstream = pl.pallas_call(
        functools.partial(block_kernel, sections, dp, chunks, 3),
        in_specs=[smem] + [vmem] * (dp + 3) + [hbm] * 2,
        out_specs=[vmem] * 4,
        out_shape=[
            like((2, tokens, hidden), BF16),
            like((dp * mp, 2 * mine, width), BF16),
            like((tokens, width), BF16),
            like((tokens, width), BF16),
        ],
        scratch_shapes=[
            pltpu.VMEM((2 * tokens, width), BF16),
            pltpu.VMEM((width, rest), BF16),
            pltpu.VMEM((width, rest), BF16),
            pltpu.VMEM((tokens, width), F32),
            pltpu.VMEM((tokens, width), F32),
            pltpu.SemaphoreType.DMA((chunks,)),
            pltpu.SemaphoreType.DMA((chunks,)),
        ],
        compiler_params=params(36),
        cost_estimate=pl.CostEstimate(
            flops=12 * tokens * width * hidden, bytes_accessed=4 * width * hidden, transcendentals=2 * tokens * hidden
        ),
        name="block",
    )(where, *rows, gain, win, wout, *stay(w_in[0], w_out[0]))

    hids = [hid] + [
        lax.ppermute(hid, "dp", [(i, (i + k) % dp) for i in range(dp)]) for k in range(1, dp)
    ]
    recv = lax.all_to_all(part, ("dp", "mp"), 0, 0)

    half = width // dp
    tile = 128 * divisor(half // 128, 2)
    grads = pl.pallas_call(
        functools.partial(weight_kernel, dp, tile),
        in_specs=[smem] + [vmem] * (2 + dp),
        out_specs=[hbm] * 2,
        out_shape=[like((half, dp * hidden), BF16)] * 2,
        scratch_shapes=[
            pltpu.VMEM((half, dp * hidden), BF16),
            pltpu.VMEM((half, dp * hidden), BF16),
            pltpu.SemaphoreType.DMA((2 * dp * (half // tile),)),
        ],
        compiler_params=params(36),
        cost_estimate=pl.CostEstimate(
            flops=4 * tokens * half * hidden * dp, bytes_accessed=4 * half * hidden * dp, transcendentals=0
        ),
        name="weight",
    )(where, n_bwd, upstream, *hids)

    act_out, grad_out = pl.pallas_call(
        functools.partial(finish_kernel, sections, mp),
        in_specs=[smem] + [vmem] * 4,
        out_specs=[vmem] * 2,
        out_shape=[like((1, mine, width), BF16)] * 2,
        compiler_params=params(16),
        name="finish",
    )(where, recv, got, saved_input, gain)
    return act_out, grad_out, grads[0][None], grads[1][None]


def solution(mesh):
    sizes = dict(mesh.shape)
    body = functools.partial(per_device, sizes["section"], sizes["dp"], sizes["mp"])
    return jax.shard_map(
        body,
        mesh=mesh,
        in_specs=(
            P("section", ("dp", "mp"), None),
            P(("dp", "mp"), None),
            P("section", ("dp", "mp"), None),
            P("section", ("dp", "mp"), None),
            P(("dp", "mp"), None),
            P("section", None),
            P("section", None, "mp"),
            P("section", None, "mp"),
        ),
        out_specs=(
            P("section", ("dp", "mp"), None),
            P("section", ("dp", "mp"), None),
            P("section", "dp", "mp"),
            P("section", "dp", "mp"),
        ),
        check_vma=False,
    )
```

```python
import functools

import jax
import jax.numpy as jnp
from jax import lax
from jax.experimental import pallas as pl
from jax.experimental.pallas import tpu as pltpu
from jax.sharding import PartitionSpec as P


GELU_C = 0.7978845608028654
BF16 = jnp.bfloat16
F32 = jnp.float32
MIB = 1 << 20


def gelu_value(h):
    tval = jnp.tanh(GELU_C * (h + 0.044715 * h * h * h))
    return 0.5 * h * (1.0 + tval)


def gelu_pair(h):
    tval = jnp.tanh(GELU_C * (h + 0.044715 * h * h * h))
    value = 0.5 * h * (1.0 + tval)
    slope = 0.5 * (1.0 + tval) + 0.5 * h * (1.0 - tval * tval) * GELU_C * (
        1.0 + 3.0 * 0.044715 * h * h
    )
    return value, slope


def normalize(xval):
    centre = xval - jnp.mean(xval, axis=-1, keepdims=True)
    rstd = lax.rsqrt(jnp.mean(centre * centre, axis=-1, keepdims=True) + 1e-05)
    return centre * rstd, rstd


def contract_last(left, right):
    return lax.dot_general(
        left, right, (((1,), (1,)), ((), ())), preferred_element_type=F32
    )


def contract_first(left, right):
    return lax.dot_general(
        left, right, (((0,), (0,)), ((), ())), preferred_element_type=F32
    )


def send_kernel(sections, mp, where_ref, act_ref, batch_ref, saved_ref, grad_ref, loss_ref, sent_ref, sems):
    section = where_ref[0]
    behind = lax.rem(section + sections - 1, sections)
    ahead = lax.rem(section + 1, sections)

    def spread(source, target, sem):
        def start(lane, carry):
            pltpu.make_async_copy(source, sent_ref.at[target * mp + lane], sems.at[sem]).start()
            return carry

        lax.fori_loop(0, mp, start, 0, unroll=mp <= 8)

    spread(saved_ref.at[0], section, 0)

    @pl.when(section == sections - 1)
    def _():
        spread(batch_ref, ahead, 1)

    @pl.when(section != sections - 1)
    def _():
        spread(act_ref.at[0], ahead, 1)

    @pl.when(section == 0)
    def _():
        spread(loss_ref, behind, 2)

    @pl.when(section != 0)
    def _():
        spread(grad_ref.at[0], behind, 2)

    for sem in range(3):
        whole = sent_ref.at[pl.ds(0, mp)]
        pltpu.make_async_copy(whole, whole, sems.at[sem]).wait()


def early_kernel(dp, where_ref, gain_hbm, win_hbm, wout_hbm, gain_ref, win_ref, wout_ref, sems):
    start = where_ref[1] * (win_hbm.shape[1] // dp)
    columns = pl.ds(pl.multiple_of(start, 128), win_ref.shape[1])
    copies = [
        pltpu.make_async_copy(win_hbm.at[:, columns], win_ref, sems.at[0]),
        pltpu.make_async_copy(gain_hbm, gain_ref, sems.at[1]),
        pltpu.make_async_copy(wout_hbm.at[:, columns], wout_ref, sems.at[2]),
    ]
    for copy in copies:
        copy.start()
    for copy in copies:
        copy.wait()


def block_kernel(sections, dp, chunks, depth, where_ref, *refs):
    rows_refs = refs[:dp]
    gain_ref, win_first, wout_first, win_hbm, wout_hbm = refs[dp : dp + 5]
    hid_ref, part_ref, norm_ref, up_ref = refs[dp + 5 : dp + 9]
    both, win, wout, branch, dnorm, sem_in, sem_out = refs[dp + 9 :]
    section, replica = where_ref[0], where_ref[1]
    lanes = rows_refs[0].shape[0] // sections
    block = lanes * rows_refs[0].shape[1]
    tokens = dp * block
    width = win_first.shape[1]
    hidden = chunks * width
    start = replica * hidden

    def fetch(chunk):
        source = pl.ds(pl.multiple_of(start + chunk * width, 128), width)
        target = pl.ds((chunk - 1) * width, width)
        return (
            pltpu.make_async_copy(win_hbm.at[:, source], win.at[:, target], sem_in.at[chunk - 1]),
            pltpu.make_async_copy(wout_hbm.at[:, source], wout.at[:, target], sem_out.at[chunk - 1]),
        )

    for chunk in range(1, min(depth + 1, chunks)):
        for copy in fetch(chunk):
            copy.start()

    behind = lax.rem(section + sections - 1, sections)
    ahead = lax.rem(section + 1, sections)
    gain = gain_ref[...]

    def rows_of(slot, owner):
        here = pl.ds(slot * lanes, lanes)
        rows = rows_refs[0][here]
        for k in range(1, dp):
            rows = jnp.where(
                lax.rem(replica + dp - k, dp) == owner, rows_refs[k][here], rows
            )
        return rows.reshape(block, rows.shape[-1])

    def weights(chunk):
        if chunk == 0:
            return win_first[...], wout_first[...]
        columns = slice((chunk - 1) * width, chunk * width)
        return win[:, columns], wout[:, columns]

    for owner in range(dp):
        low = owner * block
        nhat, _ = normalize(rows_of(behind, owner).astype(F32))
        both[low : low + block, :] = (nhat * gain).astype(BF16)
        nhat, _ = normalize(rows_of(section, owner).astype(F32))
        n_bwd = (nhat * gain).astype(BF16)
        both[tokens + low : tokens + low + block, :] = n_bwd
        norm_ref[low : low + block, :] = n_bwd
        up_ref[low : low + block, :] = rows_of(ahead, owner)

    def first(chunk):
        columns = slice(chunk * width, (chunk + 1) * width)
        if chunk > 0:
            for copy in fetch(chunk):
                copy.wait()
            if chunk + depth < chunks:
                for copy in fetch(chunk + depth):
                    copy.start()
        w_in, w_out = weights(chunk)
        h = jnp.dot(both[...], w_in, preferred_element_type=F32)
        grad_act = jnp.dot(up_ref[...], w_out, preferred_element_type=F32)
        g_fwd = gelu_value(h[:tokens]).astype(BF16)
        g_bwd, slope = gelu_pair(h[tokens:])
        dh = (grad_act * slope).astype(BF16)
        hid_ref[0, :, columns] = dh
        hid_ref[1, :, columns] = g_bwd.astype(BF16)
        return g_fwd, dh

    def second(chunk, g_fwd, dh):
        w_in, w_out = weights(chunk)
        term_n = contract_last(dh, w_in)
        term_b = contract_last(g_fwd, w_out)
        if chunk == 0:
            dnorm[...] = term_n
            branch[...] = term_b
        else:
            dnorm[...] += term_n
            branch[...] += term_b

    pending = first(0)
    for chunk in range(1, chunks):
        later = first(chunk)
        second(chunk - 1, *pending)
        pending = later
    second(chunks - 1, *pending)

    owners, mine = part_ref.shape[0], part_ref.shape[1] // 2
    for owner in range(owners):
        rows = slice(owner * mine, (owner + 1) * mine)
        part_ref[owner, :mine, :] = branch[rows, :].astype(BF16)
        part_ref[owner, mine:, :] = dnorm[rows, :].astype(BF16)


def weight_kernel(dp, tile, where_ref, norm_ref, up_ref, *refs):
    hid_refs = refs[:dp]
    targets, buffers, sems = refs[dp : dp + 2], refs[dp + 2 : dp + 4], refs[dp + 4]
    replica = where_ref[1]
    half = buffers[0].shape[0]
    hidden = hid_refs[0].shape[2]
    copies = []
    for k in range(dp):
        there = pl.ds(pl.multiple_of(lax.rem(replica + dp - k, dp) * hidden, 128), hidden)
        here = pl.ds(k * hidden, hidden)
        for step in range(half // tile):
            rows = pl.ds(step * tile, tile)
            columns = pl.ds(pl.multiple_of(replica * half + step * tile, 128), tile)
            for which, left in enumerate((norm_ref, up_ref)):
                buffer = buffers[which]
                buffer[rows, here] = contract_first(left[:, columns], hid_refs[k][which]).astype(BF16)
                copy = pltpu.make_async_copy(
                    buffer.at[rows, here], targets[which].at[rows, there], sems.at[len(copies)]
                )
                copy.start()
                copies.append(copy)
    for copy in copies:
        copy.wait()


def finish_kernel(sections, mp, where_ref, recv_ref, rows_ref, saved_ref, gain_ref, act_ref, grad_ref):
    section, lane = where_ref[0], where_ref[2]
    mine = saved_ref.shape[1]
    total = jnp.sum(recv_ref[...].astype(F32), axis=0)
    behind = lax.rem(section + sections - 1, sections) * mp + lane
    ahead = lax.rem(section + 1, sections) * mp + lane
    act_ref[0] = (rows_ref[behind].astype(F32) + total[:mine]).astype(BF16)
    nhat, rstd = normalize(saved_ref[0].astype(F32))
    scaled = total[mine:] * gain_ref[...]
    grad = rows_ref[ahead].astype(F32) + rstd * (
        scaled
        - jnp.mean(scaled, axis=-1, keepdims=True)
        - nhat * jnp.mean(scaled * nhat, axis=-1, keepdims=True)
    )
    grad_ref[0] = grad.astype(BF16)


def divisor(size, most):
    return max(k for k in range(1, most + 1) if size % k == 0)


def per_device(sections, dp, mp, act_sent, new_batch, saved_input, grad_sent, loss_grad, ln_gain, w_in, w_out):
    section = lax.axis_index("section")
    replica = lax.axis_index("dp")
    lane = lax.axis_index("mp")
    where = jnp.stack([section, replica, lane]).astype(jnp.int32)
    mine, width = new_batch.shape
    hidden = w_in.shape[2] // dp
    block = mp * mine
    tokens = dp * block
    vmem = pl.BlockSpec(memory_space=pltpu.VMEM)
    smem = pl.BlockSpec(memory_space=pltpu.SMEM)
    hbm = pl.BlockSpec(memory_space=pltpu.HBM)

    params = lambda mib: pltpu.CompilerParams(vmem_limit_bytes=mib * MIB)
    stay = lambda *arrays: [pltpu.with_memory_space_constraint(x, pltpu.HBM) for x in arrays]
    like = jax.ShapeDtypeStruct
    sent = pl.pallas_call(
        functools.partial(send_kernel, sections, mp),
        in_specs=[smem] + [hbm] * 5,
        out_specs=vmem,
        out_shape=like((sections * mp, mine, width), BF16),
        scratch_shapes=[pltpu.SemaphoreType.DMA((3,))],
        compiler_params=params(4),
        name="send",
    )(where, *stay(act_sent, new_batch, saved_input, grad_sent, loss_grad))
    got = lax.all_to_all(sent, ("section", "mp"), 0, 0)
    chunks = divisor(hidden // 128, 8)
    first = hidden // chunks
    rows = [got] + [
        lax.ppermute(got, "dp", [(i, (i + k) % dp) for i in range(dp)]) for k in range(1, dp)
    ]
    gain, win, wout = pl.pallas_call(
        functools.partial(early_kernel, dp),
        in_specs=[smem] + [hbm] * 3,
        out_specs=[vmem] * 3,
        out_shape=[
            like((1, width), F32),
            like((width, first), BF16),
            like((width, first), BF16),
        ],
        scratch_shapes=[pltpu.SemaphoreType.DMA((3,))],
        compiler_params=params(4),
        cost_estimate=pl.CostEstimate(
            flops=0, bytes_accessed=4 * width * first, transcendentals=0
        ),
        name="early",
    )(where, *stay(ln_gain, w_in[0], w_out[0]))

    rest = max(hidden - first, 128)
    hid, part, n_bwd, upstream = pl.pallas_call(
        functools.partial(block_kernel, sections, dp, chunks, 3),
        in_specs=[smem] + [vmem] * (dp + 3) + [hbm] * 2,
        out_specs=[vmem] * 4,
        out_shape=[
            like((2, tokens, hidden), BF16),
            like((dp * mp, 2 * mine, width), BF16),
            like((tokens, width), BF16),
            like((tokens, width), BF16),
        ],
        scratch_shapes=[
            pltpu.VMEM((2 * tokens, width), BF16),
            pltpu.VMEM((width, rest), BF16),
            pltpu.VMEM((width, rest), BF16),
            pltpu.VMEM((tokens, width), F32),
            pltpu.VMEM((tokens, width), F32),
            pltpu.SemaphoreType.DMA((chunks,)),
            pltpu.SemaphoreType.DMA((chunks,)),
        ],
        compiler_params=params(36),
        cost_estimate=pl.CostEstimate(
            flops=12 * tokens * width * hidden, bytes_accessed=4 * width * hidden, transcendentals=2 * tokens * hidden
        ),
        name="block",
    )(where, *rows, gain, win, wout, *stay(w_in[0], w_out[0]))

    hids = [hid] + [
        lax.ppermute(hid, "dp", [(i, (i + k) % dp) for i in range(dp)]) for k in range(1, dp)
    ]
    recv = lax.all_to_all(part, ("dp", "mp"), 0, 0)

    half = width // dp
    tile = 128 * divisor(half // 128, 2)
    grads = pl.pallas_call(
        functools.partial(weight_kernel, dp, tile),
        in_specs=[smem] + [vmem] * (2 + dp),
        out_specs=[hbm] * 2,
        out_shape=[like((half, dp * hidden), BF16)] * 2,
        scratch_shapes=[
            pltpu.VMEM((half, dp * hidden), BF16),
            pltpu.VMEM((half, dp * hidden), BF16),
            pltpu.SemaphoreType.DMA((2 * dp * (half // tile),)),
        ],
        compiler_params=params(36),
        cost_estimate=pl.CostEstimate(
            flops=4 * tokens * half * hidden * dp, bytes_accessed=4 * half * hidden * dp, transcendentals=0
        ),
        name="weight",
    )(where, n_bwd, upstream, *hids)

    act_out, grad_out = pl.pallas_call(
        functools.partial(finish_kernel, sections, mp),
        in_specs=[smem] + [vmem] * 4,
        out_specs=[vmem] * 2,
        out_shape=[like((1, mine, width), BF16)] * 2,
        compiler_params=params(16),
        name="finish",
    )(where, recv, got, saved_input, gain)
    return act_out, grad_out, grads[0][None], grads[1][None]


def solution(mesh):
    sizes = dict(mesh.shape)
    body = functools.partial(per_device, sizes["section"], sizes["dp"], sizes["mp"])
    return jax.shard_map(
        body,
        mesh=mesh,
        in_specs=(
            P("section", ("dp", "mp"), None),
            P(("dp", "mp"), None),
            P("section", ("dp", "mp"), None),
            P("section", ("dp", "mp"), None),
            P(("dp", "mp"), None),
            P("section", None),
            P("section", None, "mp"),
            P("section", None, "mp"),
        ),
        out_specs=(
            P("section", ("dp", "mp"), None),
            P("section", ("dp", "mp"), None),
            P("section", "dp", "mp"),
            P("section", "dp", "mp"),
        ),
        check_vma=False,
    )
```

```python
import functools

import jax
import jax.numpy as jnp
from jax import lax
from jax.experimental import pallas as pl
from jax.experimental.pallas import tpu as pltpu
from jax.sharding import PartitionSpec as P


GELU_C = 0.7978845608028654
BF16 = jnp.bfloat16
F32 = jnp.float32
MIB = 1 << 20


def gelu_value(h):
    tval = jnp.tanh(GELU_C * (h + 0.044715 * h * h * h))
    return 0.5 * h * (1.0 + tval)


def gelu_pair(h):
    tval = jnp.tanh(GELU_C * (h + 0.044715 * h * h * h))
    value = 0.5 * h * (1.0 + tval)
    slope = 0.5 * (1.0 + tval) + 0.5 * h * (1.0 - tval * tval) * GELU_C * (
        1.0 + 3.0 * 0.044715 * h * h
    )
    return value, slope


def normalize(xval):
    centre = xval - jnp.mean(xval, axis=-1, keepdims=True)
    rstd = lax.rsqrt(jnp.mean(centre * centre, axis=-1, keepdims=True) + 1e-05)
    return centre * rstd, rstd


def contract_last(left, right):
    return lax.dot_general(
        left, right, (((1,), (1,)), ((), ())), preferred_element_type=F32
    )


def contract_first(left, right):
    return lax.dot_general(
        left, right, (((0,), (0,)), ((), ())), preferred_element_type=F32
    )


def send_kernel(sections, dp, mp, act_ref, batch_ref, saved_ref, grad_ref, loss_ref, gain_hbm, win_hbm, wout_hbm, sent_ref, gain_ref, win_ref, wout_ref, sems, near):
    section = lax.axis_index("section")
    width = win_ref.shape[1]
    columns = pl.ds(pl.multiple_of(lax.axis_index("dp") * (win_hbm.shape[1] // dp), 128), width)
    behind = lax.rem(section + sections - 1, sections)
    ahead = lax.rem(section + 1, sections)

    def spread(source, target, sem):
        def start(lane, carry):
            pltpu.make_async_copy(source, sent_ref.at[target * mp + lane], sems.at[sem]).start()
            return carry

        lax.fori_loop(0, mp, start, 0, unroll=mp <= 8)

    spread(saved_ref.at[0], section, 0)

    @pl.when(section == sections - 1)
    def _():
        spread(batch_ref, ahead, 1)

    @pl.when(section != sections - 1)
    def _():
        spread(act_ref.at[0], ahead, 1)

    @pl.when(section == 0)
    def _():
        spread(loss_ref, behind, 2)

    @pl.when(section != 0)
    def _():
        spread(grad_ref.at[0], behind, 2)

    early = [
        pltpu.make_async_copy(gain_hbm, gain_ref, near.at[0]),
        pltpu.make_async_copy(win_hbm.at[:, columns], win_ref, near.at[1]),
        pltpu.make_async_copy(wout_hbm.at[:, columns], wout_ref, near.at[2]),
    ]
    for copy in early:
        copy.start()
    for sem in range(3):
        whole = sent_ref.at[pl.ds(0, mp)]
        pltpu.make_async_copy(whole, whole, sems.at[sem]).wait()
    for copy in early:
        copy.wait()


def block_kernel(sections, dp, chunks, depth, *refs):
    rows_refs = refs[:dp]
    gain_ref, win_first, wout_first, win_hbm, wout_hbm = refs[dp : dp + 5]
    hid_ref, part_ref, norm_ref, up_ref = refs[dp + 5 : dp + 9]
    both, win, wout, branch, dnorm, sem_in, sem_out = refs[dp + 9 :]
    section, replica = lax.axis_index("section"), lax.axis_index("dp")
    lanes = rows_refs[0].shape[0] // sections
    block = lanes * rows_refs[0].shape[1]
    tokens = dp * block
    width = win_first.shape[1]
    hidden = chunks * width
    start = replica * hidden

    def fetch(chunk):
        source = pl.ds(pl.multiple_of(start + chunk * width, 128), width)
        target = pl.ds((chunk - 1) * width, width)
        return (
            pltpu.make_async_copy(win_hbm.at[:, source], win.at[:, target], sem_in.at[chunk - 1]),
            pltpu.make_async_copy(wout_hbm.at[:, source], wout.at[:, target], sem_out.at[chunk - 1]),
        )

    for chunk in range(1, min(depth + 1, chunks)):
        for copy in fetch(chunk):
            copy.start()

    behind = lax.rem(section + sections - 1, sections)
    ahead = lax.rem(section + 1, sections)
    gain = gain_ref[...]

    def rows_of(slot, owner):
        here = pl.ds(slot * lanes, lanes)
        rows = rows_refs[0][here]
        for k in range(1, dp):
            rows = jnp.where(
                lax.rem(replica + dp - k, dp) == owner, rows_refs[k][here], rows
            )
        return rows.reshape(block, rows.shape[-1])

    def weights(chunk):
        if chunk == 0:
            return win_first[...], wout_first[...]
        columns = slice((chunk - 1) * width, chunk * width)
        return win[:, columns], wout[:, columns]

    for owner in range(dp):
        low = owner * block
        nhat, _ = normalize(rows_of(behind, owner).astype(F32))
        both[low : low + block, :] = (nhat * gain).astype(BF16)
        nhat, _ = normalize(rows_of(section, owner).astype(F32))
        n_bwd = (nhat * gain).astype(BF16)
        both[tokens + low : tokens + low + block, :] = n_bwd
        norm_ref[low : low + block, :] = n_bwd
        up_ref[low : low + block, :] = rows_of(ahead, owner)

    def first(chunk):
        columns = slice(chunk * width, (chunk + 1) * width)
        if chunk > 0:
            for copy in fetch(chunk):
                copy.wait()
            if chunk + depth < chunks:
                for copy in fetch(chunk + depth):
                    copy.start()
        w_in, w_out = weights(chunk)
        h = jnp.dot(both[...], w_in, preferred_element_type=F32)
        grad_act = jnp.dot(up_ref[...], w_out, preferred_element_type=F32)
        g_fwd = gelu_value(h[:tokens]).astype(BF16)
        g_bwd, slope = gelu_pair(h[tokens:])
        dh = (grad_act * slope).astype(BF16)
        hid_ref[0, :, columns] = dh
        hid_ref[1, :, columns] = g_bwd.astype(BF16)
        return g_fwd, dh

    def second(chunk, g_fwd, dh):
        w_in, w_out = weights(chunk)
        term_n = contract_last(dh, w_in)
        term_b = contract_last(g_fwd, w_out)
        if chunk == 0:
            dnorm[...] = term_n
            branch[...] = term_b
        else:
            dnorm[...] += term_n
            branch[...] += term_b

    pending = first(0)
    for chunk in range(1, chunks):
        later = first(chunk)
        second(chunk - 1, *pending)
        pending = later
    second(chunks - 1, *pending)

    owners, mine = part_ref.shape[0], part_ref.shape[1] // 2
    for owner in range(owners):
        rows = slice(owner * mine, (owner + 1) * mine)
        part_ref[owner, :mine, :] = branch[rows, :].astype(BF16)
        part_ref[owner, mine:, :] = dnorm[rows, :].astype(BF16)


def weight_kernel(dp, tile, norm_ref, up_ref, *refs):
    hid_refs = refs[:dp]
    targets, buffers, sems = refs[dp : dp + 2], refs[dp + 2 : dp + 4], refs[dp + 4]
    replica = lax.axis_index("dp")
    half = buffers[0].shape[0]
    hidden = hid_refs[0].shape[2]
    copies = []
    for k in range(dp):
        there = pl.ds(pl.multiple_of(lax.rem(replica + dp - k, dp) * hidden, 128), hidden)
        here = pl.ds(k * hidden, hidden)
        for step in range(half // tile):
            rows = pl.ds(step * tile, tile)
            columns = pl.ds(pl.multiple_of(replica * half + step * tile, 128), tile)
            for which, left in enumerate((norm_ref, up_ref)):
                buffer = buffers[which]
                buffer[rows, here] = contract_first(left[:, columns], hid_refs[k][which]).astype(BF16)
                copy = pltpu.make_async_copy(
                    buffer.at[rows, here], targets[which].at[rows, there], sems.at[len(copies)]
                )
                copy.start()
                copies.append(copy)
    for copy in copies:
        copy.wait()


def finish_kernel(sections, mp, recv_ref, rows_ref, saved_ref, gain_ref, act_ref, grad_ref):
    section, lane = lax.axis_index("section"), lax.axis_index("mp")
    mine = saved_ref.shape[1]
    total = jnp.sum(recv_ref[...].astype(F32), axis=0)
    behind = lax.rem(section + sections - 1, sections) * mp + lane
    ahead = lax.rem(section + 1, sections) * mp + lane
    act_ref[0] = (rows_ref[behind].astype(F32) + total[:mine]).astype(BF16)
    nhat, rstd = normalize(saved_ref[0].astype(F32))
    scaled = total[mine:] * gain_ref[...]
    grad = rows_ref[ahead].astype(F32) + rstd * (
        scaled
        - jnp.mean(scaled, axis=-1, keepdims=True)
        - nhat * jnp.mean(scaled * nhat, axis=-1, keepdims=True)
    )
    grad_ref[0] = grad.astype(BF16)


def divisor(size, most):
    return max(k for k in range(1, most + 1) if size % k == 0)


def per_device(sections, dp, mp, act_sent, new_batch, saved_input, grad_sent, loss_grad, ln_gain, w_in, w_out):
    mine, width = new_batch.shape
    hidden = w_in.shape[2] // dp
    block = mp * mine
    tokens = dp * block
    vmem = pl.BlockSpec(memory_space=pltpu.VMEM)
    hbm = pl.BlockSpec(memory_space=pltpu.HBM)

    params = lambda mib: pltpu.CompilerParams(vmem_limit_bytes=mib * MIB)
    stay = lambda *arrays: [pltpu.with_memory_space_constraint(x, pltpu.HBM) for x in arrays]
    like = jax.ShapeDtypeStruct
    chunks = divisor(hidden // 128, 8)
    first = hidden // chunks
    sent, gain, win, wout = pl.pallas_call(
        functools.partial(send_kernel, sections, dp, mp),
        in_specs=[hbm] * 8,
        out_specs=[vmem] * 4,
        out_shape=[
            like((sections * mp, mine, width), BF16),
            like((1, width), F32),
            like((width, first), BF16),
            like((width, first), BF16),
        ],
        scratch_shapes=[pltpu.SemaphoreType.DMA((3,)), pltpu.SemaphoreType.DMA((3,))],
        compiler_params=params(4),
        name="send",
    )(*stay(act_sent, new_batch, saved_input, grad_sent, loss_grad, ln_gain, w_in[0], w_out[0]))
    got = lax.all_to_all(sent, ("section", "mp"), 0, 0)
    rows = [got] + [
        lax.ppermute(got, "dp", [(i, (i + k) % dp) for i in range(dp)]) for k in range(1, dp)
    ]

    rest = max(hidden - first, 128)
    hid, part, n_bwd, upstream = pl.pallas_call(
        functools.partial(block_kernel, sections, dp, chunks, 3),
        in_specs=[vmem] * (dp + 3) + [hbm] * 2,
        out_specs=[vmem] * 4,
        out_shape=[
            like((2, tokens, hidden), BF16),
            like((dp * mp, 2 * mine, width), BF16),
            like((tokens, width), BF16),
            like((tokens, width), BF16),
        ],
        scratch_shapes=[
            pltpu.VMEM((2 * tokens, width), BF16),
            pltpu.VMEM((width, rest), BF16),
            pltpu.VMEM((width, rest), BF16),
            pltpu.VMEM((tokens, width), F32),
            pltpu.VMEM((tokens, width), F32),
            pltpu.SemaphoreType.DMA((chunks,)),
            pltpu.SemaphoreType.DMA((chunks,)),
        ],
        compiler_params=params(36),
        cost_estimate=pl.CostEstimate(
            flops=12 * tokens * width * hidden, bytes_accessed=4 * width * hidden, transcendentals=2 * tokens * hidden
        ),
        name="block",
    )(*rows, gain, win, wout, *stay(w_in[0], w_out[0]))

    hids = [hid] + [
        lax.ppermute(hid, "dp", [(i, (i + k) % dp) for i in range(dp)]) for k in range(1, dp)
    ]
    recv = lax.all_to_all(part, ("dp", "mp"), 0, 0)

    half = width // dp
    tile = 128 * divisor(half // 128, 2)
    grads = pl.pallas_call(
        functools.partial(weight_kernel, dp, tile),
        in_specs=[vmem] * (2 + dp),
        out_specs=[hbm] * 2,
        out_shape=[like((half, dp * hidden), BF16)] * 2,
        scratch_shapes=[
            pltpu.VMEM((half, dp * hidden), BF16),
            pltpu.VMEM((half, dp * hidden), BF16),
            pltpu.SemaphoreType.DMA((2 * dp * (half // tile),)),
        ],
        compiler_params=params(36),
        cost_estimate=pl.CostEstimate(
            flops=4 * tokens * half * hidden * dp, bytes_accessed=4 * half * hidden * dp, transcendentals=0
        ),
        name="weight",
    )(n_bwd, upstream, *hids)

    act_out, grad_out = pl.pallas_call(
        functools.partial(finish_kernel, sections, mp),
        in_specs=[vmem] * 4,
        out_specs=[vmem] * 2,
        out_shape=[like((1, mine, width), BF16)] * 2,
        compiler_params=params(16),
        name="finish",
    )(recv, got, saved_input, gain)
    return act_out, grad_out, grads[0][None], grads[1][None]


def solution(mesh):
    sizes = dict(mesh.shape)
    body = functools.partial(per_device, sizes["section"], sizes["dp"], sizes["mp"])
    return jax.shard_map(
        body,
        mesh=mesh,
        in_specs=(
            P("section", ("dp", "mp"), None),
            P(("dp", "mp"), None),
            P("section", ("dp", "mp"), None),
            P("section", ("dp", "mp"), None),
            P(("dp", "mp"), None),
            P("section", None),
            P("section", None, "mp"),
            P("section", None, "mp"),
        ),
        out_specs=(
            P("section", ("dp", "mp"), None),
            P("section", ("dp", "mp"), None),
            P("section", "dp", "mp"),
            P("section", "dp", "mp"),
        ),
        check_vma=False,
    )
```

```python
import functools

import jax
import jax.numpy as jnp
from jax import lax
from jax.experimental import pallas as pl
from jax.experimental.pallas import tpu as pltpu
from jax.sharding import PartitionSpec as P


GELU_C = 0.7978845608028654
BF16 = jnp.bfloat16
F32 = jnp.float32
MIB = 1 << 20


def gelu_value(h):
    tval = jnp.tanh(GELU_C * (h + 0.044715 * h * h * h))
    return 0.5 * h * (1.0 + tval)


def gelu_pair(h):
    tval = jnp.tanh(GELU_C * (h + 0.044715 * h * h * h))
    value = 0.5 * h * (1.0 + tval)
    slope = 0.5 * (1.0 + tval) + 0.5 * h * (1.0 - tval * tval) * GELU_C * (
        1.0 + 3.0 * 0.044715 * h * h
    )
    return value, slope


def normalize(xval):
    centre = xval - jnp.mean(xval, axis=-1, keepdims=True)
    rstd = lax.rsqrt(jnp.mean(centre * centre, axis=-1, keepdims=True) + 1e-05)
    return centre * rstd, rstd


def contract_last(left, right):
    return lax.dot_general(
        left, right, (((1,), (1,)), ((), ())), preferred_element_type=F32
    )


def contract_first(left, right):
    return lax.dot_general(
        left, right, (((0,), (0,)), ((), ())), preferred_element_type=F32
    )


def send_kernel(sections, mp, act_ref, batch_ref, saved_ref, grad_ref, loss_ref, sent_ref, sems):
    section = lax.axis_index("section")
    behind = lax.rem(section + sections - 1, sections)
    ahead = lax.rem(section + 1, sections)

    def spread(source, target, sem):
        def start(lane, carry):
            pltpu.make_async_copy(source, sent_ref.at[target * mp + lane], sems.at[sem]).start()
            return carry

        lax.fori_loop(0, mp, start, 0, unroll=mp <= 8)

    spread(saved_ref.at[0], section, 0)

    @pl.when(section == sections - 1)
    def _():
        spread(batch_ref, ahead, 1)

    @pl.when(section != sections - 1)
    def _():
        spread(act_ref.at[0], ahead, 1)

    @pl.when(section == 0)
    def _():
        spread(loss_ref, behind, 2)

    @pl.when(section != 0)
    def _():
        spread(grad_ref.at[0], behind, 2)

    for sem in range(3):
        whole = sent_ref.at[pl.ds(0, mp)]
        pltpu.make_async_copy(whole, whole, sems.at[sem]).wait()


def early_kernel(dp, gain_hbm, win_hbm, wout_hbm, gain_ref, win_ref, wout_ref, sems):
    start = lax.axis_index("dp") * (win_hbm.shape[1] // dp)
    columns = pl.ds(pl.multiple_of(start, 128), win_ref.shape[1])
    copies = [
        pltpu.make_async_copy(win_hbm.at[:, columns], win_ref, sems.at[0]),
        pltpu.make_async_copy(gain_hbm, gain_ref, sems.at[1]),
        pltpu.make_async_copy(wout_hbm.at[:, columns], wout_ref, sems.at[2]),
    ]
    for copy in copies:
        copy.start()
    for copy in copies:
        copy.wait()


def block_kernel(sections, dp, chunks, depth, *refs):
    rows_refs = refs[:dp]
    gain_ref, win_first, wout_first, win_hbm, wout_hbm = refs[dp : dp + 5]
    hid_ref, part_ref, norm_ref, up_ref = refs[dp + 5 : dp + 9]
    both, win, wout, branch, dnorm, sem_in, sem_out = refs[dp + 9 :]
    section, replica = lax.axis_index("section"), lax.axis_index("dp")
    lanes = rows_refs[0].shape[0] // sections
    block = lanes * rows_refs[0].shape[1]
    tokens = dp * block
    width = win_first.shape[1]
    hidden = chunks * width
    start = replica * hidden

    def fetch(chunk):
        source = pl.ds(pl.multiple_of(start + chunk * width, 128), width)
        target = pl.ds((chunk - 1) * width, width)
        return (
            pltpu.make_async_copy(win_hbm.at[:, source], win.at[:, target], sem_in.at[chunk - 1]),
            pltpu.make_async_copy(wout_hbm.at[:, source], wout.at[:, target], sem_out.at[chunk - 1]),
        )

    for chunk in range(1, min(depth + 1, chunks)):
        for copy in fetch(chunk):
            copy.start()

    behind = lax.rem(section + sections - 1, sections)
    ahead = lax.rem(section + 1, sections)
    gain = gain_ref[...]

    def rows_of(slot, owner):
        here = pl.ds(slot * lanes, lanes)
        rows = rows_refs[0][here]
        for k in range(1, dp):
            rows = jnp.where(
                lax.rem(replica + dp - k, dp) == owner, rows_refs[k][here], rows
            )
        return rows.reshape(block, rows.shape[-1])

    def weights(chunk):
        if chunk == 0:
            return win_first[...], wout_first[...]
        columns = slice((chunk - 1) * width, chunk * width)
        return win[:, columns], wout[:, columns]

    for owner in range(dp):
        low = owner * block
        nhat, _ = normalize(rows_of(behind, owner).astype(F32))
        both[low : low + block, :] = (nhat * gain).astype(BF16)
        nhat, _ = normalize(rows_of(section, owner).astype(F32))
        n_bwd = (nhat * gain).astype(BF16)
        both[tokens + low : tokens + low + block, :] = n_bwd
        norm_ref[low : low + block, :] = n_bwd
        up_ref[low : low + block, :] = rows_of(ahead, owner)

    def first(chunk):
        columns = slice(chunk * width, (chunk + 1) * width)
        if chunk > 0:
            for copy in fetch(chunk):
                copy.wait()
            if chunk + depth < chunks:
                for copy in fetch(chunk + depth):
                    copy.start()
        w_in, w_out = weights(chunk)
        h = jnp.dot(both[...], w_in, preferred_element_type=F32)
        grad_act = jnp.dot(up_ref[...], w_out, preferred_element_type=F32)
        g_fwd = gelu_value(h[:tokens]).astype(BF16)
        g_bwd, slope = gelu_pair(h[tokens:])
        dh = (grad_act * slope).astype(BF16)
        hid_ref[0, :, columns] = dh
        hid_ref[1, :, columns] = g_bwd.astype(BF16)
        return g_fwd, dh

    def second(chunk, g_fwd, dh):
        w_in, w_out = weights(chunk)
        term_n = contract_last(dh, w_in)
        term_b = contract_last(g_fwd, w_out)
        if chunk == 0:
            dnorm[...] = term_n
            branch[...] = term_b
        else:
            dnorm[...] += term_n
            branch[...] += term_b

    pending = first(0)
    for chunk in range(1, chunks):
        later = first(chunk)
        second(chunk - 1, *pending)
        pending = later
    second(chunks - 1, *pending)

    owners, mine = part_ref.shape[0], part_ref.shape[1] // 2
    for owner in range(owners):
        rows = slice(owner * mine, (owner + 1) * mine)
        part_ref[owner, :mine, :] = branch[rows, :].astype(BF16)
        part_ref[owner, mine:, :] = dnorm[rows, :].astype(BF16)


def weight_kernel(dp, tile, norm_ref, up_ref, *refs):
    hid_refs = refs[:dp]
    targets, buffers, sems = refs[dp : dp + 2], refs[dp + 2 : dp + 4], refs[dp + 4]
    replica = lax.axis_index("dp")
    half = buffers[0].shape[0]
    hidden = hid_refs[0].shape[2]
    copies = []
    for k in range(dp):
        there = pl.ds(pl.multiple_of(lax.rem(replica + dp - k, dp) * hidden, 128), hidden)
        here = pl.ds(k * hidden, hidden)
        for step in range(half // tile):
            rows = pl.ds(step * tile, tile)
            columns = pl.ds(pl.multiple_of(replica * half + step * tile, 128), tile)
            for which, left in enumerate((norm_ref, up_ref)):
                buffer = buffers[which]
                buffer[rows, here] = contract_first(left[:, columns], hid_refs[k][which]).astype(BF16)
                copy = pltpu.make_async_copy(
                    buffer.at[rows, here], targets[which].at[rows, there], sems.at[len(copies)]
                )
                copy.start()
                copies.append(copy)
    for copy in copies:
        copy.wait()


def finish_kernel(sections, mp, recv_ref, rows_ref, saved_ref, gain_ref, act_ref, grad_ref):
    section, lane = lax.axis_index("section"), lax.axis_index("mp")
    mine = saved_ref.shape[1]
    total = jnp.sum(recv_ref[...].astype(F32), axis=0)
    behind = lax.rem(section + sections - 1, sections) * mp + lane
    ahead = lax.rem(section + 1, sections) * mp + lane
    act_ref[0] = (rows_ref[behind].astype(F32) + total[:mine]).astype(BF16)
    nhat, rstd = normalize(saved_ref[0].astype(F32))
    scaled = total[mine:] * gain_ref[...]
    grad = rows_ref[ahead].astype(F32) + rstd * (
        scaled
        - jnp.mean(scaled, axis=-1, keepdims=True)
        - nhat * jnp.mean(scaled * nhat, axis=-1, keepdims=True)
    )
    grad_ref[0] = grad.astype(BF16)


def divisor(size, most):
    return max(k for k in range(1, most + 1) if size % k == 0)


def per_device(sections, dp, mp, act_sent, new_batch, saved_input, grad_sent, loss_grad, ln_gain, w_in, w_out):
    mine, width = new_batch.shape
    hidden = w_in.shape[2] // dp
    block = mp * mine
    tokens = dp * block
    vmem = pl.BlockSpec(memory_space=pltpu.VMEM)
    hbm = pl.BlockSpec(memory_space=pltpu.HBM)

    params = lambda mib: pltpu.CompilerParams(vmem_limit_bytes=mib * MIB)
    stay = lambda *arrays: [pltpu.with_memory_space_constraint(x, pltpu.HBM) for x in arrays]
    like = jax.ShapeDtypeStruct
    sent = pl.pallas_call(
        functools.partial(send_kernel, sections, mp),
        in_specs=[hbm] * 5,
        out_specs=vmem,
        out_shape=like((sections * mp, mine, width), BF16),
        scratch_shapes=[pltpu.SemaphoreType.DMA((3,))],
        compiler_params=params(4),
        name="send",
    )(*stay(act_sent, new_batch, saved_input, grad_sent, loss_grad))
    got = lax.all_to_all(sent, ("section", "mp"), 0, 0)
    chunks = divisor(hidden // 128, 8)
    first = hidden // chunks
    rows = [got] + [
        lax.ppermute(got, "dp", [(i, (i + k) % dp) for i in range(dp)]) for k in range(1, dp)
    ]
    gain, win, wout = pl.pallas_call(
        functools.partial(early_kernel, dp),
        in_specs=[hbm] * 3,
        out_specs=[vmem] * 3,
        out_shape=[
            like((1, width), F32),
            like((width, first), BF16),
            like((width, first), BF16),
        ],
        scratch_shapes=[pltpu.SemaphoreType.DMA((3,))],
        compiler_params=params(4),
        cost_estimate=pl.CostEstimate(
            flops=0, bytes_accessed=4 * width * first, transcendentals=0
        ),
        name="early",
    )(*stay(ln_gain, w_in[0], w_out[0]))

    rest = max(hidden - first, 128)
    hid, part, n_bwd, upstream = pl.pallas_call(
        functools.partial(block_kernel, sections, dp, chunks, 3),
        in_specs=[vmem] * (dp + 3) + [hbm] * 2,
        out_specs=[vmem] * 4,
        out_shape=[
            like((2, tokens, hidden), BF16),
            like((dp * mp, 2 * mine, width), BF16),
            like((tokens, width), BF16),
            like((tokens, width), BF16),
        ],
        scratch_shapes=[
            pltpu.VMEM((2 * tokens, width), BF16),
            pltpu.VMEM((width, rest), BF16),
            pltpu.VMEM((width, rest), BF16),
            pltpu.VMEM((tokens, width), F32),
            pltpu.VMEM((tokens, width), F32),
            pltpu.SemaphoreType.DMA((chunks,)),
            pltpu.SemaphoreType.DMA((chunks,)),
        ],
        compiler_params=params(36),
        cost_estimate=pl.CostEstimate(
            flops=12 * tokens * width * hidden, bytes_accessed=4 * width * hidden, transcendentals=2 * tokens * hidden
        ),
        name="block",
    )(*rows, gain, win, wout, *stay(w_in[0], w_out[0]))

    hids = [hid] + [
        lax.ppermute(hid, "dp", [(i, (i + k) % dp) for i in range(dp)]) for k in range(1, dp)
    ]
    recv = lax.all_to_all(part, ("dp", "mp"), 0, 0)

    half = width // dp
    tile = 128 * divisor(half // 128, 2)
    grads = pl.pallas_call(
        functools.partial(weight_kernel, dp, tile),
        in_specs=[vmem] * (2 + dp),
        out_specs=[hbm] * 2,
        out_shape=[like((half, dp * hidden), BF16)] * 2,
        scratch_shapes=[
            pltpu.VMEM((half, dp * hidden), BF16),
            pltpu.VMEM((half, dp * hidden), BF16),
            pltpu.SemaphoreType.DMA((2 * dp * (half // tile),)),
        ],
        compiler_params=params(36),
        cost_estimate=pl.CostEstimate(
            flops=4 * tokens * half * hidden * dp, bytes_accessed=4 * half * hidden * dp, transcendentals=0
        ),
        name="weight",
    )(n_bwd, upstream, *hids)

    act_out, grad_out = pl.pallas_call(
        functools.partial(finish_kernel, sections, mp),
        in_specs=[vmem] * 4,
        out_specs=[vmem] * 2,
        out_shape=[like((1, mine, width), BF16)] * 2,
        compiler_params=params(16),
        name="finish",
    )(recv, got, saved_input, gain)
    return act_out, grad_out, grads[0][None], grads[1][None]


def solution(mesh):
    sizes = dict(mesh.shape)
    body = functools.partial(per_device, sizes["section"], sizes["dp"], sizes["mp"])
    return jax.shard_map(
        body,
        mesh=mesh,
        in_specs=(
            P("section", ("dp", "mp"), None),
            P(("dp", "mp"), None),
            P("section", ("dp", "mp"), None),
            P("section", ("dp", "mp"), None),
            P(("dp", "mp"), None),
            P("section", None),
            P("section", None, "mp"),
            P("section", None, "mp"),
        ),
        out_specs=(
            P("section", ("dp", "mp"), None),
            P("section", ("dp", "mp"), None),
            P("section", "dp", "mp"),
            P("section", "dp", "mp"),
        ),
        check_vma=False,
    )
```

```python
import functools

import jax
import jax.numpy as jnp
from jax import lax
from jax.experimental import pallas as pl
from jax.experimental.pallas import tpu as pltpu
from jax.sharding import PartitionSpec as P


GELU_C = 0.7978845608028654
BF16 = jnp.bfloat16
F32 = jnp.float32
MIB = 1 << 20


def gelu_value(h):
    tval = jnp.tanh(GELU_C * (h + 0.044715 * h * h * h))
    return 0.5 * h * (1.0 + tval)


def gelu_pair(h):
    tval = jnp.tanh(GELU_C * (h + 0.044715 * h * h * h))
    value = 0.5 * h * (1.0 + tval)
    slope = 0.5 * (1.0 + tval) + 0.5 * h * (1.0 - tval * tval) * GELU_C * (
        1.0 + 3.0 * 0.044715 * h * h
    )
    return value, slope


def normalize(xval):
    centre = xval - jnp.mean(xval, axis=-1, keepdims=True)
    rstd = lax.rsqrt(jnp.mean(centre * centre, axis=-1, keepdims=True) + 1e-05)
    return centre * rstd, rstd


def contract_last(left, right):
    return lax.dot_general(
        left, right, (((1,), (1,)), ((), ())), preferred_element_type=F32
    )


def contract_first(left, right):
    return lax.dot_general(
        left, right, (((0,), (0,)), ((), ())), preferred_element_type=F32
    )


def send_kernel(sections, mp, act_ref, batch_ref, saved_ref, grad_ref, loss_ref, sent_ref, sems):
    section = lax.axis_index("section")
    behind = lax.rem(section + sections - 1, sections)
    ahead = lax.rem(section + 1, sections)

    def spread(source, target, sem):
        def start(lane, carry):
            pltpu.make_async_copy(source, sent_ref.at[lane, target], sems.at[sem]).start()
            return carry

        lax.fori_loop(0, mp, start, 0, unroll=mp <= 8)

    spread(saved_ref.at[0], section, 0)

    @pl.when(section == sections - 1)
    def _():
        spread(batch_ref, ahead, 1)

    @pl.when(section != sections - 1)
    def _():
        spread(act_ref.at[0], ahead, 1)

    @pl.when(section == 0)
    def _():
        spread(loss_ref, behind, 2)

    @pl.when(section != 0)
    def _():
        spread(grad_ref.at[0], behind, 2)

    for sem in range(3):
        whole = sent_ref.at[:, 0]
        pltpu.make_async_copy(whole, whole, sems.at[sem]).wait()


def early_kernel(dp, gain_hbm, win_hbm, wout_hbm, gain_ref, win_ref, wout_ref, sems):
    start = lax.axis_index("dp") * (win_hbm.shape[1] // dp)
    columns = pl.ds(pl.multiple_of(start, 128), win_ref.shape[1])
    copies = [
        pltpu.make_async_copy(win_hbm.at[:, columns], win_ref, sems.at[0]),
        pltpu.make_async_copy(gain_hbm, gain_ref, sems.at[1]),
        pltpu.make_async_copy(wout_hbm.at[:, columns], wout_ref, sems.at[2]),
    ]
    for copy in copies:
        copy.start()
    for copy in copies:
        copy.wait()


def block_kernel(sections, dp, chunks, depth, *refs):
    rows_refs = refs[:dp]
    gain_ref, win_first, wout_first, win_hbm, wout_hbm = refs[dp : dp + 5]
    hid_ref, part_ref, norm_ref, up_ref = refs[dp + 5 : dp + 9]
    both, win, wout, branch, dnorm, sem_in, sem_out = refs[dp + 9 :]
    section, replica = lax.axis_index("section"), lax.axis_index("dp")
    block = rows_refs[0].shape[0] * rows_refs[0].shape[2]
    tokens = dp * block
    width = win_first.shape[1]
    hidden = chunks * width
    start = replica * hidden

    def fetch(chunk):
        source = pl.ds(pl.multiple_of(start + chunk * width, 128), width)
        target = pl.ds((chunk - 1) * width, width)
        return (
            pltpu.make_async_copy(win_hbm.at[:, source], win.at[:, target], sem_in.at[chunk - 1]),
            pltpu.make_async_copy(wout_hbm.at[:, source], wout.at[:, target], sem_out.at[chunk - 1]),
        )

    for chunk in range(1, min(depth + 1, chunks)):
        for copy in fetch(chunk):
            copy.start()

    behind = lax.rem(section + sections - 1, sections)
    ahead = lax.rem(section + 1, sections)
    gain = gain_ref[...]

    def rows_of(slot, owner):
        rows = rows_refs[0][:, slot]
        for k in range(1, dp):
            rows = jnp.where(
                lax.rem(replica + dp - k, dp) == owner, rows_refs[k][:, slot], rows
            )
        return rows.reshape(block, rows.shape[-1])

    def weights(chunk):
        if chunk == 0:
            return win_first[...], wout_first[...]
        columns = slice((chunk - 1) * width, chunk * width)
        return win[:, columns], wout[:, columns]

    for owner in range(dp):
        low = owner * block
        nhat, _ = normalize(rows_of(behind, owner).astype(F32))
        both[low : low + block, :] = (nhat * gain).astype(BF16)
        nhat, _ = normalize(rows_of(section, owner).astype(F32))
        n_bwd = (nhat * gain).astype(BF16)
        both[tokens + low : tokens + low + block, :] = n_bwd
        norm_ref[low : low + block, :] = n_bwd
        up_ref[low : low + block, :] = rows_of(ahead, owner)

    def first(chunk):
        columns = slice(chunk * width, (chunk + 1) * width)
        if chunk > 0:
            for copy in fetch(chunk):
                copy.wait()
            if chunk + depth < chunks:
                for copy in fetch(chunk + depth):
                    copy.start()
        w_in, w_out = weights(chunk)
        h = jnp.dot(both[...], w_in, preferred_element_type=F32)
        grad_act = jnp.dot(up_ref[...], w_out, preferred_element_type=F32)
        g_fwd = gelu_value(h[:tokens]).astype(BF16)
        g_bwd, slope = gelu_pair(h[tokens:])
        dh = (grad_act * slope).astype(BF16)
        hid_ref[0, :, columns] = dh
        hid_ref[1, :, columns] = g_bwd.astype(BF16)
        return g_fwd, dh

    def second(chunk, g_fwd, dh):
        w_in, w_out = weights(chunk)
        term_n = contract_last(dh, w_in)
        term_b = contract_last(g_fwd, w_out)
        if chunk == 0:
            dnorm[...] = term_n
            branch[...] = term_b
        else:
            dnorm[...] += term_n
            branch[...] += term_b

    pending = first(0)
    for chunk in range(1, chunks):
        later = first(chunk)
        second(chunk - 1, *pending)
        pending = later
    second(chunks - 1, *pending)

    owners, mine = part_ref.shape[0], part_ref.shape[1] // 2
    for owner in range(owners):
        rows = slice(owner * mine, (owner + 1) * mine)
        part_ref[owner, :mine, :] = branch[rows, :].astype(BF16)
        part_ref[owner, mine:, :] = dnorm[rows, :].astype(BF16)


def weight_kernel(dp, tile, norm_ref, up_ref, *refs):
    hid_refs = refs[:dp]
    targets, buffers, sems = refs[dp : dp + 2], refs[dp + 2 : dp + 4], refs[dp + 4]
    replica = lax.axis_index("dp")
    half = buffers[0].shape[0]
    hidden = hid_refs[0].shape[2]
    copies = []
    for k in range(dp):
        there = pl.ds(pl.multiple_of(lax.rem(replica + dp - k, dp) * hidden, 128), hidden)
        here = pl.ds(k * hidden, hidden)
        for step in range(half // tile):
            rows = pl.ds(step * tile, tile)
            columns = pl.ds(pl.multiple_of(replica * half + step * tile, 128), tile)
            for which, left in enumerate((norm_ref, up_ref)):
                buffer = buffers[which]
                buffer[rows, here] = contract_first(left[:, columns], hid_refs[k][which]).astype(BF16)
                copy = pltpu.make_async_copy(
                    buffer.at[rows, here], targets[which].at[rows, there], sems.at[len(copies)]
                )
                copy.start()
                copies.append(copy)
    for copy in copies:
        copy.wait()


def finish_kernel(sections, recv_ref, rows_ref, saved_ref, gain_ref, act_ref, grad_ref):
    section, lane = lax.axis_index("section"), lax.axis_index("mp")
    mine = saved_ref.shape[1]
    total = jnp.sum(recv_ref[...].astype(F32), axis=0)
    behind = lax.rem(section + sections - 1, sections)
    ahead = lax.rem(section + 1, sections)
    act_ref[0] = (rows_ref[lane, behind].astype(F32) + total[:mine]).astype(BF16)
    nhat, rstd = normalize(saved_ref[0].astype(F32))
    scaled = total[mine:] * gain_ref[...]
    grad = rows_ref[lane, ahead].astype(F32) + rstd * (
        scaled
        - jnp.mean(scaled, axis=-1, keepdims=True)
        - nhat * jnp.mean(scaled * nhat, axis=-1, keepdims=True)
    )
    grad_ref[0] = grad.astype(BF16)


def divisor(size, most):
    return max(k for k in range(1, most + 1) if size % k == 0)


def per_device(sections, dp, mp, act_sent, new_batch, saved_input, grad_sent, loss_grad, ln_gain, w_in, w_out):
    mine, width = new_batch.shape
    hidden = w_in.shape[2] // dp
    block = mp * mine
    tokens = dp * block
    vmem = pl.BlockSpec(memory_space=pltpu.VMEM)
    hbm = pl.BlockSpec(memory_space=pltpu.HBM)

    params = lambda mib: pltpu.CompilerParams(vmem_limit_bytes=mib * MIB)
    stay = lambda *arrays: [pltpu.with_memory_space_constraint(x, pltpu.HBM) for x in arrays]
    like = jax.ShapeDtypeStruct
    sent = pl.pallas_call(
        functools.partial(send_kernel, sections, mp),
        in_specs=[hbm] * 5,
        out_specs=vmem,
        out_shape=like((mp, sections, mine, width), BF16),
        scratch_shapes=[pltpu.SemaphoreType.DMA((3,))],
        compiler_params=params(4),
        name="send",
    )(*stay(act_sent, new_batch, saved_input, grad_sent, loss_grad))
    got = lax.all_to_all(sent.reshape(mp * sections, mine, width), ("mp", "section"), 0, 0)
    got = got.reshape(mp, sections, mine, width)
    chunks = divisor(hidden // 128, 8)
    first = hidden // chunks
    rows = [got] + [
        lax.ppermute(got, "dp", [(i, (i + k) % dp) for i in range(dp)]) for k in range(1, dp)
    ]
    gain, win, wout = pl.pallas_call(
        functools.partial(early_kernel, dp),
        in_specs=[hbm] * 3,
        out_specs=[vmem] * 3,
        out_shape=[
            like((1, width), F32),
            like((width, first), BF16),
            like((width, first), BF16),
        ],
        scratch_shapes=[pltpu.SemaphoreType.DMA((3,))],
        compiler_params=params(4),
        cost_estimate=pl.CostEstimate(
            flops=0, bytes_accessed=4 * width * first, transcendentals=0
        ),
        name="early",
    )(*stay(ln_gain, w_in[0], w_out[0]))

    rest = max(hidden - first, 128)
    hid, part, n_bwd, upstream = pl.pallas_call(
        functools.partial(block_kernel, sections, dp, chunks, 3),
        in_specs=[vmem] * (dp + 3) + [hbm] * 2,
        out_specs=[vmem] * 4,
        out_shape=[
            like((2, tokens, hidden), BF16),
            like((dp * mp, 2 * mine, width), BF16),
            like((tokens, width), BF16),
            like((tokens, width), BF16),
        ],
        scratch_shapes=[
            pltpu.VMEM((2 * tokens, width), BF16),
            pltpu.VMEM((width, rest), BF16),
            pltpu.VMEM((width, rest), BF16),
            pltpu.VMEM((tokens, width), F32),
            pltpu.VMEM((tokens, width), F32),
            pltpu.SemaphoreType.DMA((chunks,)),
            pltpu.SemaphoreType.DMA((chunks,)),
        ],
        compiler_params=params(36),
        cost_estimate=pl.CostEstimate(
            flops=12 * tokens * width * hidden, bytes_accessed=4 * width * hidden, transcendentals=2 * tokens * hidden
        ),
        name="block",
    )(*rows, gain, win, wout, *stay(w_in[0], w_out[0]))

    hids = [hid] + [
        lax.ppermute(hid, "dp", [(i, (i + k) % dp) for i in range(dp)]) for k in range(1, dp)
    ]
    recv = lax.all_to_all(part, ("dp", "mp"), 0, 0)

    half = width // dp
    tile = 128 * divisor(half // 128, 2)
    grads = pl.pallas_call(
        functools.partial(weight_kernel, dp, tile),
        in_specs=[vmem] * (2 + dp),
        out_specs=[hbm] * 2,
        out_shape=[like((half, dp * hidden), BF16)] * 2,
        scratch_shapes=[
            pltpu.VMEM((half, dp * hidden), BF16),
            pltpu.VMEM((half, dp * hidden), BF16),
            pltpu.SemaphoreType.DMA((2 * dp * (half // tile),)),
        ],
        compiler_params=params(36),
        cost_estimate=pl.CostEstimate(
            flops=4 * tokens * half * hidden * dp, bytes_accessed=4 * half * hidden * dp, transcendentals=0
        ),
        name="weight",
    )(n_bwd, upstream, *hids)

    act_out, grad_out = pl.pallas_call(
        functools.partial(finish_kernel, sections),
        in_specs=[vmem] * 4,
        out_specs=[vmem] * 2,
        out_shape=[like((1, mine, width), BF16)] * 2,
        compiler_params=params(16),
        name="finish",
    )(recv, got, saved_input, gain)
    return act_out, grad_out, grads[0][None], grads[1][None]


def solution(mesh):
    sizes = dict(mesh.shape)
    body = functools.partial(per_device, sizes["section"], sizes["dp"], sizes["mp"])
    return jax.shard_map(
        body,
        mesh=mesh,
        in_specs=(
            P("section", ("dp", "mp"), None),
            P(("dp", "mp"), None),
            P("section", ("dp", "mp"), None),
            P("section", ("dp", "mp"), None),
            P(("dp", "mp"), None),
            P("section", None),
            P("section", None, "mp"),
            P("section", None, "mp"),
        ),
        out_specs=(
            P("section", ("dp", "mp"), None),
            P("section", ("dp", "mp"), None),
            P("section", "dp", "mp"),
            P("section", "dp", "mp"),
        ),
        check_vma=False,
    )
```
